256 devices in a mesh: segment: 4 (over x), dp: 64 (over y, z, core).
Axes of the slice: x: 4, y: 4, z: 8, core: 2. Of those that a mesh axis runs over, the one named last changes fastest.
Arguments:
- activations: bfloat16 [4, 512, 4, 4, 8, 256], P('segment', 'dp'), may hold values from -6 to 6
- preacts: bfloat16 [4, 512, 4, 4, 8, 256], P('segment', 'dp'), may hold values from -10 to 10
- out_grad: bfloat16 [512, 4, 4, 8, 256], P('dp'), may hold values from -6 to 6
- weights: float32 [4, 256, 27, 256], P('segment', 'dp'), may hold values from -0.078125 to 0.078125
- momentum: float32 [4, 256, 27, 256], P('segment', 'dp'), may hold values from -6 to 6
- noise: float32 [4, 256, 27, 256], P('segment', 'dp'), may hold values from -6 to 6
Outputs:
- new_momentum: float32 [4, 256, 27, 256], P('segment', 'dp')
The draws below stay inside these ranges and needn't reach their ends.
All inputs are finite; a program needn't handle non-finite values.
Results may differ from the reference program's by a relative error of at most 0.0033.
Values may be sent and summed in bfloat16 or wider, within the bound.
A program may use at most 192 MiB of HBM per device.

```python
import math
import jax
import jax.numpy as jnp
from jax import lax

C = 256
TAPS = 27
CT = 4
CX = 4
CY = 8
MICRO = 8
CELLS = 128
SAMP = 512
SEGMENTS = 4
N_DP = 64


def steps_of(stream_key, shape, cuts, least, largest):
    def one(dim, shards_of):
        heights = jax.random.uniform(jax.random.fold_in(jax.random.fold_in(stream_key, 6), dim), (shards_of,), jnp.float32, least / len(cuts), largest / len(cuts))
        return jnp.repeat(jnp.exp(heights), shape[dim] // shards_of).reshape((-1,) + (1,) * (len(shape) - dim - 1))

    loudness = one(*cuts[0])
    for cut in cuts[1:]:
        loudness = loudness * one(*cut)
    return loudness


def bell_draw(own_key, shape, scale, bound, shards=(), kind=jnp.bfloat16):
    factor_of = steps_of(own_key, shape, shards, -0.22, 0.18) if shards else 1.0
    drawn = jax.random.normal(own_key, shape, jnp.float32) * scale * factor_of
    return jnp.minimum(jnp.maximum(drawn, -bound), bound).astype(kind)


def setup_inputs(seed: int = 0) -> dict:
    key_of = jax.random.split(jax.random.key(seed), 7)
    return {
        "activations": bell_draw(key_of[0], (SEGMENTS, SAMP, CT, CX, CY, C), 1.0, 6.0, ((0, 4), (1, 64))),
        "preacts": bell_draw(key_of[1], (SEGMENTS, SAMP, CT, CX, CY, C), 2.0, 10.0, ((0, 4), (1, 64))),
        "out_grad": bell_draw(key_of[2], (SAMP, CT, CX, CY, C), 1.0, 6.0, ((0, 64),)),
        "weights": bell_draw(key_of[3], (SEGMENTS, C, TAPS, C), (C * TAPS) ** -0.5, 0.078125, ((0, 4), (1, 64)), jnp.float32),
        "momentum": bell_draw(key_of[4], (SEGMENTS, C, TAPS, C), 1.0, 6.0, ((0, 4), (1, 64)), jnp.float32),
        "noise": bell_draw(key_of[5], (SEGMENTS, C, TAPS, C), 1.0, 6.0, ((0, 4), (1, 64)), jnp.float32),
    }


def tap_stack(field, sign):
    batch_n, span_t, span_x, span_y, channels = field.shape
    padded = jnp.pad(field, ((0, 0), (1, 1), (1, 1), (1, 1), (0, 0)))
    views = []
    for along_t in (-1, 0, 1):
        for along_x in (-1, 0, 1):
            for along_y in (-1, 0, 1):
                start_t = 1 + sign * along_t
                start_x = 1 + sign * along_x
                start_y = 1 + sign * along_y
                views.append(padded[:, start_t:start_t + span_t, start_x:start_x + span_x, start_y:start_y + span_y, :])
    return jnp.stack(views, axis=4).reshape(batch_n * span_t * span_x * span_y, 27, channels)

def reference(activations, preacts, out_grad, weights, momentum, noise):
    segments = activations.shape[0]
    crop_shape = activations.shape[2:]
    grads = []
    upstream_all = out_grad
    for segment in range(segments - 1, -1, -1):
        rounded = lax.optimization_barrier(weights[segment].astype(jnp.bfloat16))
        kernel = rounded.astype(jnp.float32)
        group_in = activations[segment].reshape((N_DP, MICRO) + crop_shape)
        group_pre = preacts[segment].reshape((N_DP, MICRO) + crop_shape)
        group_up = upstream_all.reshape((N_DP, MICRO) + crop_shape)

        def group_step(total, pieces):
            inputs, pres, upstream = pieces
            pre = pres.astype(jnp.float32)
            sig = jax.nn.sigmoid(pre)
            up_wide = upstream.astype(jnp.float32)
            grad_pre = (up_wide * sig * (1.0 + pre * (1.0 - sig))).astype(jnp.bfloat16)
            pre_cols = tap_stack(grad_pre, -1).astype(jnp.float32)
            back = jnp.einsum('nto,cto->nc', pre_cols, kernel)
            passed = (up_wide + back.reshape(upstream.shape)).astype(jnp.bfloat16)
            in_cols = tap_stack(inputs, 1).astype(jnp.float32)
            flat_pre = grad_pre.reshape(-1, C).astype(jnp.float32)
            total = total + jnp.einsum('ntc,no->cto', in_cols, flat_pre)
            return (total, passed)
        total, passed = lax.scan(group_step, jnp.zeros((C, TAPS, C), jnp.float32), (group_in, group_pre, group_up))
        grads.append(total)
        upstream_all = passed.reshape(out_grad.shape)
    grads = jnp.stack(grads[::-1])
    rate = 1.0 / math.sqrt(SAMP * CELLS)
    return 0.9 * momentum - rate * grads + 0.3 * noise
```

```python
import functools
import math

import jax
import jax.numpy as jnp
from jax import lax
from jax.experimental import pallas as pl
from jax.experimental.pallas import tpu as pltpu
from jax.sharding import PartitionSpec as P

MESH = pl.DeviceIdType.MESH
F32 = jnp.float32
BF16 = jnp.bfloat16

NSEG = 4
NY = 4
NZ = 8
C = 256
ROWS = 4
MICRO = 8
G = 2
NG = MICRO // G
RG = G * 128
MSG = 112
HALF = 64
NK = 9
Z_ORDER = (0, 1, 7, 2, 6, 3, 5, 4)


def iota(axis, shape=(256, 256)):
    return lax.broadcasted_iota(jnp.int32, shape, axis)


def dot(a, b, ca, cb):
    return lax.dot_general(a, b, (((ca,), (cb,)), ((), ())), preferred_element_type=F32)


def body(
    wt, act, pre, og, out,
    wtmp, W, K, D, Q, XT, up, upsend,
    own1, sb1, rb1, sap, sam, rap, ram, sbp, sbm, rbp, rbm, zf, zown, zs, zr,
    s_z, r_z, s_yp, r_yp, s_ym, r_ym, s_hp, r_hp, s_hm, r_hm, s_sib, r_sib,
    s_x, r_x, s_1, r_1, s_ap, r_ap, s_am, r_am, s_bp, r_bp, s_bm, r_bm, s_3, r_3,
):
    seg = lax.axis_index("segment")
    dp = lax.axis_index("dp")
    y = dp // 16
    z = (dp // 2) % 8
    c = dp % 2

    def at(yy, zz, cc):
        return (seg, yy * 16 + zz * 2 + cc)

    yp = at((y + 1) % NY, z, c)
    ym = at((y + 3) % NY, z, c)
    sib = at(y, z, 1 - c)

    def zpeer(d):
        return at(y, (z + d) % NZ, c)

    def rc(src, dst, ss, rs, dev):
        return pltpu.make_async_remote_copy(
            src_ref=src, dst_ref=dst, send_sem=ss, recv_sem=rs, device_id=dev, device_id_type=MESH
        )

    barrier = pltpu.get_barrier_semaphore()
    peers = [yp, ym, sib] + [zpeer(d) for d in range(1, NZ)]
    peers += [((seg + 1) % NSEG, dp), ((seg + NSEG - 1) % NSEG, dp)]
    for dev in peers:
        pl.semaphore_signal(barrier, inc=1, device_id=dev, device_id_type=MESH)

    wtmp[104:112, :] = jnp.zeros((8, C), F32)
    for t in range(27):
        wtmp[4 * t : 4 * t + 4, :] = wt[t]
    W[z, c, y] = wtmp[...].astype(BF16)

    pl.semaphore_wait(barrier, len(peers))

    def cp_z(d):
        piece = W.at[z, c, y]
        return rc(piece, piece, s_z.at[d], r_z.at[d], zpeer(d))

    def in_z(d):
        piece = W.at[(z + 8 - d) % NZ, c, y]
        return rc(piece, piece, s_z.at[d], r_z.at[d], zpeer(d))

    def cp_yp(d, src=None):
        piece = W.at[(z + 8 - d) % NZ, c, y if src is None else src]
        return rc(piece, piece, s_yp.at[d], r_yp.at[d], yp)

    def cp_ym(d, src=None):
        piece = W.at[(z + 8 - d) % NZ, c, y if src is None else src]
        return rc(piece, piece, s_ym.at[d], r_ym.at[d], ym)

    def cp_hp(d, src):
        piece = W.at[(z + 8 - d) % NZ, c, src, pl.ds(0, HALF)]
        return rc(piece, piece, s_hp.at[d], r_hp.at[d], yp)

    def cp_hm(d, src):
        piece = W.at[(z + 8 - d) % NZ, c, src, pl.ds(HALF, MSG - HALF)]
        return rc(piece, piece, s_hm.at[d], r_hm.at[d], ym)

    def cp_sib(d, cc):
        piece = W.at[(z + 8 - d) % NZ, cc]
        return rc(piece, piece, s_sib.at[d], r_sib.at[d], sib)

    up_of = (y + 1) % NY
    down_of = (y + 3) % NY
    far = (y + 2) % NY

    cp_yp(0).start()
    cp_ym(0).start()
    for d in Z_ORDER[1:]:
        cp_z(d).start()

    Q[:, :, 0] = jnp.zeros((9, MICRO, 32, C), BF16)
    Q[:, :, 5] = jnp.zeros((9, MICRO, 32, C), BF16)

    def derivative(i, carry):
        rows = pl.ds(pl.multiple_of(i * 128, 128), 128)
        p = pre[rows, :].astype(F32)
        sig = jax.nn.sigmoid(p)
        D[rows, :] = sig * (1.0 + p * (1.0 - sig))
        return carry

    row = iota(0)
    ch = (
        ((y + ((row >> 5) & 3)) & 3) * 64
        + ((z + ((row >> 2) & 7)) & 7) * 8
        + ((c + (row >> 7)) & 1) * 4
        + (row & 3)
    )
    pick = jnp.where(iota(1) == ch, 1.0, 0.0).astype(BF16)
    XT[...] = dot(pick, act[...], 1, 1).astype(BF16)

    lag = len(Z_ORDER)
    for j in range(lag + 4):
        if j < lag:
            d = Z_ORDER[j]
            if d != 0:
                in_z(d).wait_recv()
                cp_yp(d).start()
                cp_ym(d).start()
        if j == 0:
            lax.fori_loop(0, MICRO, derivative, 0)
        if 0 <= j - 2 < lag:
            d = Z_ORDER[j - 2]
            cp_yp(d, down_of).wait_recv()
            cp_hp(d, down_of).start()
            cp_ym(d, up_of).wait_recv()
            cp_hm(d, up_of).start()
        if 0 <= j - 4 < lag:
            d = Z_ORDER[j - 4]
            cp_hp(d, far).wait_recv()
            cp_hm(d, far).wait_recv()
            cp_sib(d, c).start()
    for d in Z_ORDER:
        cp_sib(d, 1 - c).wait_recv()

    @pl.when(seg > 0)
    def _():
        r = iota(0)
        src = ((r >> 3) & 1) * 128 + ((r >> 2) & 1) * 64 + ((r >> 4) & 3) * 16 + (r >> 6) * 4 + (r & 3)
        order = jnp.where(iota(1) == src, 1.0, 0.0).astype(BF16)

        def assemble(zp, carry):
            for q in range(7):
                b = W[pl.ds(2 * zp, 2), :, :, 16 * q : 16 * q + 16, :].reshape(256, C)
                m = dot(order, b, 1, 0).astype(BF16)
                for tap in range(4):
                    for yy in range(NY):
                        K[4 * q + tap, pl.ds(pl.multiple_of(64 * yy + 16 * zp, 16), 16), :] = m[
                            64 * tap + 16 * yy : 64 * tap + 16 * yy + 16
                        ]
            return carry

        lax.fori_loop(0, 4, assemble, 0)

    def hop(g):
        return rc(upsend.at[g], up.at[g], s_x.at[g], r_x.at[g], (jnp.maximum(seg - 1, 0), dp))

    def hop_in(g):
        return rc(upsend.at[g], up.at[g], s_x.at[g], r_x.at[g], (jnp.maximum(seg - 1, 0), dp))

    def pipe(g, carry):
        rows = pl.ds(pl.multiple_of(g * RG, RG), RG)

        @pl.when(seg == NSEG - 1)
        def _():
            up[g] = og[rows, :]

        @pl.when(seg < NSEG - 1)
        def _():
            hop_in(g).wait_recv()

        u = up[g].astype(F32)
        gp = (u * D[rows, :]).astype(BF16).astype(F32)
        cell_y = iota(0, (RG, C)) & 7
        zero = jnp.zeros((4 * G, 8, C), F32)
        for oy in (-1, 0, 1):
            if oy == 1:
                s = jnp.where(cell_y == 0, 0.0, pltpu.roll(gp, 1, 0))
            elif oy == -1:
                s = jnp.where(cell_y == 7, 0.0, pltpu.roll(gp, RG - 1, 0))
            else:
                s = gp
            s = s.reshape(4 * G, 32, C)
            for ox in (-1, 0, 1):
                if ox == 1:
                    v = jnp.concatenate([zero, s[:, :24]], axis=1)
                elif ox == -1:
                    v = jnp.concatenate([s[:, 8:], zero], axis=1)
                else:
                    v = s
                Q[3 * (ox + 1) + oy + 1, pl.ds(G * g, G), 1:5] = v.reshape(G, 4, 32, C).astype(BF16)

        @pl.when(seg > 0)
        def _():
            total = u
            for k in range(NK):
                for a in range(3):
                    q = Q[k, pl.ds(G * g, G), 2 - a : 6 - a].reshape(RG, C)
                    total = total + dot(q, K[9 * a + k], 1, 1)
            upsend[g] = total.astype(BF16)
            hop(g).start()

        return carry

    lax.fori_loop(0, NG, pipe, 0)

    def cp_1(k):
        return rc(sb1.at[k], rb1.at[k], s_1.at[k], r_1.at[k], sib)

    def cp_ap(k):
        return rc(sap.at[k], rap.at[k], s_ap.at[k], r_ap.at[k], yp)

    def cp_am(k):
        return rc(sam.at[k], ram.at[k], s_am.at[k], r_am.at[k], ym)

    def cp_bp(k):
        return rc(sbp.at[k], rbp.at[k], s_bp.at[k], r_bp.at[k], yp)

    def cp_bm(k):
        return rc(sbm.at[k], rbm.at[k], s_bm.at[k], r_bm.at[k], ym)

    def cp_3(k, d):
        return rc(zs.at[k, d], zr.at[k, d], s_3.at[k, d], r_3.at[k, d], zpeer(d))

    for d in range(NZ):
        zf[d, 8:16, :] = jnp.zeros((8, C), F32)

    def stage_a(k):
        for a in range(3):
            g = dot(XT[...], Q[k, :, 2 - a : 6 - a].reshape(1024, C), 1, 0)
            own1[k, a] = g[:128]
            sb1[k, a] = g[128:].astype(BF16)
        cp_1(k).start()

    def stage_b(k):
        cp_1(k).wait_recv()
        total = own1[k] + rb1[k].astype(F32)
        own1[k] = total
        sap[k] = total[:, 64:96, :128].astype(BF16)
        sam[k] = total[:, 64:96, 128:].astype(BF16)
        cp_ap(k).start()
        cp_am(k).start()

    def stage_c(k):
        cp_ap(k).wait_recv()
        cp_am(k).wait_recv()
        sbp[k, :, :, :128] = (own1[k, :, 32:64, :128] + rap[k].astype(F32)).astype(BF16)
        sbp[k, :, :, 128:] = own1[k, :, 32:64, 128:].astype(BF16)
        sbm[k, :, :, :128] = own1[k, :, 96:128, :128].astype(BF16)
        sbm[k, :, :, 128:] = (own1[k, :, 96:128, 128:] + ram[k].astype(F32)).astype(BF16)
        cp_bp(k).start()
        cp_bm(k).start()

    def stage_d(k):
        cp_bp(k).wait_recv()
        cp_bm(k).wait_recv()
        for a in range(3):
            ys = own1[k, a, 0:32] + rbp[k, a].astype(F32) + rbm[k, a].astype(F32)
            for d in range(NZ):
                zf[d, 4 * a : 4 * a + 4, :] = ys[4 * d : 4 * d + 4]
        zown[k] = zf[0]
        zs[k] = zf[...].astype(BF16)
        for d in range(1, NZ):
            cp_3(k, d).start()

    def step(i, carry):
        for lead, stage in ((6, stage_d), (4, stage_c), (2, stage_b), (0, stage_a)):
            k = i - lead

            @pl.when(jnp.logical_and(k >= 0, k < NK))
            def _():
                stage(k)

        return carry

    lax.fori_loop(0, NK + 6, step, 0)

    def finish(k, carry):
        total = zown[k]
        for d in range(1, NZ):
            cp_3(k, d).wait_recv()
            total = total + zr[k, d].astype(F32)
        for a in range(3):
            out[9 * a + k] = total[4 * a : 4 * a + 4]
        return carry

    lax.fori_loop(0, NK, finish, 0)

    for d in range(NZ):
        if d > 0:
            cp_z(d).wait_send()
        cp_yp(d).wait_send()
        cp_ym(d).wait_send()
        cp_hp(d, down_of).wait_send()
        cp_hm(d, up_of).wait_send()
        cp_sib(d, c).wait_send()

    @pl.when(seg > 0)
    def _():
        for g in range(NG):
            hop(g).wait_send()

    def drain(k, carry):
        for cp in (cp_1, cp_ap, cp_am, cp_bp, cp_bm):
            cp(k).wait_send()
        for d in range(1, NZ):
            cp_3(k, d).wait_send()
        return carry

    lax.fori_loop(0, NK, drain, 0)


def gradient(wt, act, pre, og):
    vmem = pltpu.VMEM
    dma = pltpu.SemaphoreType.DMA
    scratch = [
        vmem((MSG, C), F32),
        vmem((NZ, 2, NY, MSG, C), BF16),
        vmem((28, C, C), BF16),
        vmem((MICRO * 128, C), F32),
        vmem((9, MICRO, 6, 32, C), BF16),
        vmem((C, MICRO * 128), BF16),
        vmem((NG, RG, C), BF16),
        vmem((NG, RG, C), BF16),
        vmem((NK, 3, 128, C), F32),
        vmem((NK, 3, 128, C), BF16),
        vmem((NK, 3, 128, C), BF16),
    ]
    scratch += [vmem((NK, 3, 32, 128), BF16)] * 4
    scratch += [vmem((NK, 3, 32, C), BF16)] * 4
    scratch += [
        vmem((NZ, 16, C), F32),
        vmem((NK, 16, C), F32),
        vmem((NK, NZ, 16, C), BF16),
        vmem((NK, NZ, 16, C), BF16),
    ]
    scratch += [dma((NZ,))] * 12
    scratch += [dma((NG,))] * 2
    scratch += [dma((NK,))] * 10
    scratch += [dma((NK, NZ))] * 2
    return pl.pallas_call(
        body,
        out_shape=jax.ShapeDtypeStruct((27, ROWS, C), F32),
        in_specs=[pl.BlockSpec(memory_space=pltpu.VMEM)] * 4,
        out_specs=pl.BlockSpec(memory_space=pltpu.VMEM),
        scratch_shapes=scratch,
        compiler_params=pltpu.CompilerParams(
            collective_id=0, has_side_effects=True, vmem_limit_bytes=56 << 20
        ),
    )(wt, act, pre, og)


def shards(activations, preacts, out_grad, weights, momentum, noise):
    cells = MICRO * 128
    grads = gradient(
        weights[0].transpose(1, 0, 2),
        activations.reshape(cells, C),
        preacts.reshape(cells, C),
        out_grad.reshape(cells, C),
    ).transpose(1, 0, 2)
    rate = 1.0 / math.sqrt(lax.axis_size("dp") * cells)
    updated = 0.9 * momentum[0] - rate * grads + 0.3 * noise[0]
    return updated[None]


def solution(mesh):
    placed = (
        P("segment", "dp", None, None, None, None),
        P("segment", "dp", None, None, None, None),
        P("dp", None, None, None, None),
        P("segment", "dp", None, None),
        P("segment", "dp", None, None),
        P("segment", "dp", None, None),
    )
    return jax.shard_map(
        shards,
        mesh=mesh,
        in_specs=placed,
        out_specs=P("segment", "dp", None, None),
        check_vma=False,
    )
```

```python
import functools
import math

import jax
import jax.numpy as jnp
from jax import lax
from jax.experimental import pallas as pl
from jax.experimental.pallas import tpu as pltpu
from jax.sharding import PartitionSpec as P

MESH = pl.DeviceIdType.MESH
F32 = jnp.float32
BF16 = jnp.bfloat16

NSEG = 4
NY = 4
NZ = 8
C = 256
ROWS = 4
MICRO = 8
G = 1
NG = MICRO // G
RG = G * 128
MSG = 112
HALF = 64
LAG_B, LAG_C, LAG_D = 2, 5, 9
NK = 9
Z_ORDER = (0, 1, 7, 2, 6, 3, 5, 4)


def iota(axis, shape=(256, 256)):
    return lax.broadcasted_iota(jnp.int32, shape, axis)


def dot(a, b, ca, cb):
    return lax.dot_general(a, b, (((ca,), (cb,)), ((), ())), preferred_element_type=F32)


def body(
    wt, act, pre, og, out,
    wtmp, W, K, D, Q, XT, up, upsend,
    own1, sb1, rb1, sap, sam, rap, ram, sbp, sbm, rbp, rbm, zf, zown, zs, zr,
    s_z, r_z, s_yp, r_yp, s_ym, r_ym, s_hp, r_hp, s_hm, r_hm, s_sib, r_sib,
    s_x, r_x, s_1, r_1, s_ap, r_ap, s_am, r_am, s_bp, r_bp, s_bm, r_bm, s_3, r_3,
):
    seg = lax.axis_index("segment")
    dp = lax.axis_index("dp")
    y = dp // 16
    z = (dp // 2) % 8
    c = dp % 2

    def at(yy, zz, cc):
        return (seg, yy * 16 + zz * 2 + cc)

    yp = at((y + 1) % NY, z, c)
    ym = at((y + 3) % NY, z, c)
    sib = at(y, z, 1 - c)

    def zpeer(d):
        return at(y, (z + d) % NZ, c)

    def rc(src, dst, ss, rs, dev):
        return pltpu.make_async_remote_copy(
            src_ref=src, dst_ref=dst, send_sem=ss, recv_sem=rs, device_id=dev, device_id_type=MESH
        )

    barrier = pltpu.get_barrier_semaphore()
    peers = [yp, ym, sib] + [zpeer(d) for d in range(1, NZ)]
    peers += [((seg + 1) % NSEG, dp), ((seg + NSEG - 1) % NSEG, dp)]
    for dev in peers:
        pl.semaphore_signal(barrier, inc=1, device_id=dev, device_id_type=MESH)

    wtmp[104:112, :] = jnp.zeros((8, C), F32)
    for t in range(27):
        wtmp[4 * t : 4 * t + 4, :] = wt[t]
    W[z, c, y] = wtmp[...].astype(BF16)

    Q[:, :, 0] = jnp.zeros((9, MICRO, 32, C), BF16)
    Q[:, :, 5] = jnp.zeros((9, MICRO, 32, C), BF16)

    def derivative(i, carry):
        rows = pl.ds(pl.multiple_of(i * 128, 128), 128)
        p = pre[rows, :].astype(F32)
        sig = jax.nn.sigmoid(p)
        D[rows, :] = sig * (1.0 + p * (1.0 - sig))
        return carry

    row = iota(0)
    ch = (
        ((y + ((row >> 5) & 3)) & 3) * 64
        + ((z + ((row >> 2) & 7)) & 7) * 8
        + ((c + (row >> 7)) & 1) * 4
        + (row & 3)
    )
    pick = jnp.where(iota(1) == ch, 1.0, 0.0).astype(BF16)
    XT[...] = dot(pick, act[...], 1, 1).astype(BF16)
    lax.fori_loop(0, MICRO, derivative, 0)

    pl.semaphore_wait(barrier, len(peers))

    def cp_z(d):
        up_z = d <= 4
        src = (z + 8 - (d - 1)) % NZ if up_z else (z + 7 - d) % NZ
        piece = W.at[src, c, y]
        return rc(piece, piece, s_z.at[d], r_z.at[d], zpeer(1 if up_z else 7))

    def in_z(d):
        piece = W.at[(z + 8 - d) % NZ, c, y]
        return rc(piece, piece, s_z.at[d], r_z.at[d], zpeer(1))

    def cp_yp(d, src=None):
        piece = W.at[(z + 8 - d) % NZ, c, y if src is None else src]
        return rc(piece, piece, s_yp.at[d], r_yp.at[d], yp)

    def cp_ym(d, src=None):
        piece = W.at[(z + 8 - d) % NZ, c, y if src is None else src]
        return rc(piece, piece, s_ym.at[d], r_ym.at[d], ym)

    def cp_hp(d, src):
        piece = W.at[(z + 8 - d) % NZ, c, src, pl.ds(0, HALF)]
        return rc(piece, piece, s_hp.at[d], r_hp.at[d], yp)

    def cp_hm(d, src):
        piece = W.at[(z + 8 - d) % NZ, c, src, pl.ds(HALF, MSG - HALF)]
        return rc(piece, piece, s_hm.at[d], r_hm.at[d], ym)

    def cp_sib(d, cc):
        piece = W.at[(z + 8 - d) % NZ, cc]
        return rc(piece, piece, s_sib.at[d], r_sib.at[d], sib)

    up_of = (y + 1) % NY
    down_of = (y + 3) % NY
    far = (y + 2) % NY

    cp_yp(0).start()
    cp_ym(0).start()
    cp_z(1).start()
    cp_z(7).start()

    lag = len(Z_ORDER)
    for j in range(lag + 4):
        if j < lag:
            d = Z_ORDER[j]
            if d != 0:
                in_z(d).wait_recv()
                if d < 4:
                    cp_z(d + 1).start()
                elif d > 5:
                    cp_z(d - 1).start()
                cp_yp(d).start()
                cp_ym(d).start()
        if 0 <= j - 2 < lag:
            d = Z_ORDER[j - 2]
            cp_yp(d, down_of).wait_recv()
            cp_hp(d, down_of).start()
            cp_ym(d, up_of).wait_recv()
            cp_hm(d, up_of).start()
        if 0 <= j - 4 < lag:
            d = Z_ORDER[j - 4]
            cp_hp(d, far).wait_recv()
            cp_hm(d, far).wait_recv()
            cp_sib(d, c).start()
    r = iota(0)
    src = ((r >> 3) & 1) * 128 + ((r >> 2) & 1) * 64 + ((r >> 4) & 3) * 16 + (r >> 6) * 4 + (r & 3)
    order = jnp.where(iota(1) == src, 1.0, 0.0).astype(BF16)

    def assemble(zp):
        for q in range(7):
            b = W[pl.ds(2 * zp, 2), :, :, 16 * q : 16 * q + 16, :].reshape(256, C)
            m = dot(order, b, 1, 0).astype(BF16)
            for tap in range(4):
                for yy in range(NY):
                    K[4 * q + tap, pl.ds(pl.multiple_of(64 * yy + 16 * zp, 16), 16), :] = m[
                        64 * tap + 16 * yy : 64 * tap + 16 * yy + 16
                    ]

    half_z = z // 2
    for needed, pair in (((0, 1, 7), 0), ((2, 3), 3), ((6, 5), 1), ((4,), 2)):
        for d in needed:
            cp_sib(d, 1 - c).wait_recv()

        @pl.when(seg > 0)
        def _():
            assemble((half_z + pair) % 4)

    def hop(g):
        return rc(upsend.at[g], up.at[g], s_x.at[g], r_x.at[g], (jnp.maximum(seg - 1, 0), dp))

    def hop_in(g):
        return rc(upsend.at[g], up.at[g], s_x.at[g], r_x.at[g], (jnp.maximum(seg - 1, 0), dp))

    def pipe(g, carry):
        rows = pl.ds(pl.multiple_of(g * RG, RG), RG)

        @pl.when(seg == NSEG - 1)
        def _():
            up[g] = og[rows, :]

        @pl.when(seg < NSEG - 1)
        def _():
            hop_in(g).wait_recv()

        u = up[g].astype(F32)
        gp = (u * D[rows, :]).astype(BF16).astype(F32)
        cell_y = iota(0, (RG, C)) & 7
        zero = jnp.zeros((4 * G, 8, C), F32)
        for oy in (-1, 0, 1):
            if oy == 1:
                s = jnp.where(cell_y == 0, 0.0, pltpu.roll(gp, 1, 0))
            elif oy == -1:
                s = jnp.where(cell_y == 7, 0.0, pltpu.roll(gp, RG - 1, 0))
            else:
                s = gp
            s = s.reshape(4 * G, 32, C)
            for ox in (-1, 0, 1):
                if ox == 1:
                    v = jnp.concatenate([zero, s[:, :24]], axis=1)
                elif ox == -1:
                    v = jnp.concatenate([s[:, 8:], zero], axis=1)
                else:
                    v = s
                Q[3 * (ox + 1) + oy + 1, pl.ds(G * g, G), 1:5] = v.reshape(G, 4, 32, C).astype(BF16)

        @pl.when(seg > 0)
        def _():
            total = u
            for k in range(NK):
                for a in range(3):
                    q = Q[k, pl.ds(G * g, G), 2 - a : 6 - a].reshape(RG, C)
                    total = total + dot(q, K[9 * a + k], 1, 1)
            upsend[g] = total.astype(BF16)
            hop(g).start()

        return carry

    lax.fori_loop(0, NG, pipe, 0)

    def cp_1(k):
        return rc(sb1.at[k], rb1.at[k], s_1.at[k], r_1.at[k], sib)

    def cp_ap(k):
        return rc(sap.at[k], rap.at[k], s_ap.at[k], r_ap.at[k], yp)

    def cp_am(k):
        return rc(sam.at[k], ram.at[k], s_am.at[k], r_am.at[k], ym)

    def cp_bp(k):
        return rc(sbp.at[k], rbp.at[k], s_bp.at[k], r_bp.at[k], yp)

    def cp_bm(k):
        return rc(sbm.at[k], rbm.at[k], s_bm.at[k], r_bm.at[k], ym)

    def cp_3(k, d):
        return rc(zs.at[k, d], zr.at[k, d], s_3.at[k, d], r_3.at[k, d], zpeer(d))

    for d in range(NZ):
        zf[d, 8:16, :] = jnp.zeros((8, C), F32)

    def stage_a(k):
        for a in range(3):
            g = dot(XT[...], Q[k, :, 2 - a : 6 - a].reshape(1024, C), 1, 0)
            own1[k, a] = g[:128]
            sb1[k, a] = g[128:].astype(BF16)
        cp_1(k).start()

    def stage_b(k):
        cp_1(k).wait_recv()
        total = own1[k] + rb1[k].astype(F32)
        own1[k] = total
        sap[k] = total[:, 64:96, :128].astype(BF16)
        sam[k] = total[:, 64:96, 128:].astype(BF16)
        cp_ap(k).start()
        cp_am(k).start()

    def stage_c(k):
        cp_ap(k).wait_recv()
        cp_am(k).wait_recv()
        sbp[k, :, :, :128] = (own1[k, :, 32:64, :128] + rap[k].astype(F32)).astype(BF16)
        sbp[k, :, :, 128:] = own1[k, :, 32:64, 128:].astype(BF16)
        sbm[k, :, :, :128] = own1[k, :, 96:128, :128].astype(BF16)
        sbm[k, :, :, 128:] = (own1[k, :, 96:128, 128:] + ram[k].astype(F32)).astype(BF16)
        cp_bp(k).start()
        cp_bm(k).start()

    def stage_d(k):
        cp_bp(k).wait_recv()
        cp_bm(k).wait_recv()
        for a in range(3):
            ys = own1[k, a, 0:32] + rbp[k, a].astype(F32) + rbm[k, a].astype(F32)
            for d in range(NZ):
                zf[d, 4 * a : 4 * a + 4, :] = ys[4 * d : 4 * d + 4]
        zown[k] = zf[0]
        zs[k] = zf[...].astype(BF16)
        for d in range(1, NZ):
            cp_3(k, d).start()

    def step(i, carry):
        for lead, stage in ((LAG_D, stage_d), (LAG_C, stage_c), (LAG_B, stage_b), (0, stage_a)):
            k = i - lead

            @pl.when(jnp.logical_and(k >= 0, k < NK))
            def _():
                stage(k)

        return carry

    lax.fori_loop(0, NK + LAG_D, step, 0)

    def finish(k, carry):
        total = zown[k]
        for d in range(1, NZ):
            cp_3(k, d).wait_recv()
            total = total + zr[k, d].astype(F32)
        for a in range(3):
            out[9 * a + k] = total[4 * a : 4 * a + 4]
        return carry

    lax.fori_loop(0, NK, finish, 0)

    for d in range(NZ):
        if d > 0:
            cp_z(d).wait_send()
        cp_yp(d).wait_send()
        cp_ym(d).wait_send()
        cp_hp(d, down_of).wait_send()
        cp_hm(d, up_of).wait_send()
        cp_sib(d, c).wait_send()

    @pl.when(seg > 0)
    def _():
        for g in range(NG):
            hop(g).wait_send()

    def drain(k, carry):
        for cp in (cp_1, cp_ap, cp_am, cp_bp, cp_bm):
            cp(k).wait_send()
        for d in range(1, NZ):
            cp_3(k, d).wait_send()
        return carry

    lax.fori_loop(0, NK, drain, 0)


def gradient(wt, act, pre, og):
    vmem = pltpu.VMEM
    dma = pltpu.SemaphoreType.DMA
    scratch = [
        vmem((MSG, C), F32),
        vmem((NZ, 2, NY, MSG, C), BF16),
        vmem((28, C, C), BF16),
        vmem((MICRO * 128, C), F32),
        vmem((9, MICRO, 6, 32, C), BF16),
        vmem((C, MICRO * 128), BF16),
        vmem((NG, RG, C), BF16),
        vmem((NG, RG, C), BF16),
        vmem((NK, 3, 128, C), F32),
        vmem((NK, 3, 128, C), BF16),
        vmem((NK, 3, 128, C), BF16),
    ]
    scratch += [vmem((NK, 3, 32, 128), BF16)] * 4
    scratch += [vmem((NK, 3, 32, C), BF16)] * 4
    scratch += [
        vmem((NZ, 16, C), F32),
        vmem((NK, 16, C), F32),
        vmem((NK, NZ, 16, C), BF16),
        vmem((NK, NZ, 16, C), BF16),
    ]
    scratch += [dma((NZ,))] * 12
    scratch += [dma((NG,))] * 2
    scratch += [dma((NK,))] * 10
    scratch += [dma((NK, NZ))] * 2
    return pl.pallas_call(
        body,
        out_shape=jax.ShapeDtypeStruct((27, ROWS, C), F32),
        in_specs=[pl.BlockSpec(memory_space=pltpu.VMEM)] * 4,
        out_specs=pl.BlockSpec(memory_space=pltpu.VMEM),
        scratch_shapes=scratch,
        compiler_params=pltpu.CompilerParams(
            collective_id=0, has_side_effects=True, vmem_limit_bytes=56 << 20
        ),
    )(wt, act, pre, og)


def shards(activations, preacts, out_grad, weights, momentum, noise):
    cells = MICRO * 128
    grads = gradient(
        weights[0].transpose(1, 0, 2),
        activations.reshape(cells, C),
        preacts.reshape(cells, C),
        out_grad.reshape(cells, C),
    ).transpose(1, 0, 2)
    rate = 1.0 / math.sqrt(lax.axis_size("dp") * cells)
    updated = 0.9 * momentum[0] - rate * grads + 0.3 * noise[0]
    return updated[None]


def solution(mesh):
    placed = (
        P("segment", "dp", None, None, None, None),
        P("segment", "dp", None, None, None, None),
        P("dp", None, None, None, None),
        P("segment", "dp", None, None),
        P("segment", "dp", None, None),
        P("segment", "dp", None, None),
    )
    return jax.shard_map(
        shards,
        mesh=mesh,
        in_specs=placed,
        out_specs=P("segment", "dp", None, None),
        check_vma=False,
    )
```

```python
import functools
import math

import jax
import jax.numpy as jnp
from jax import lax
from jax.experimental import pallas as pl
from jax.experimental.pallas import tpu as pltpu
from jax.sharding import PartitionSpec as P

MESH = pl.DeviceIdType.MESH
F32 = jnp.float32
BF16 = jnp.bfloat16

NSEG = 4
NY = 4
NZ = 8
C = 256
ROWS = 4
MICRO = 8
G = 1
NG = MICRO // G
RG = G * 128
MSG = 112
Z_HOPS = {
    1: (0, 1, 0, 0), 7: (0, 7, 0, 0), 2: (0, 2, 0, 0), 6: (0, 6, 0, 0), 3: (1, 2, 0, 0), 5: (7, 6, 0, 0),
    4: (2, 2, 1, 1), 12: (6, 6, 2, 2),
}
SPLIT = 112
LAG_B, LAG_C, LAG_D = 2, 5, 9

Z_GROUPS = ((0, 2), (2, 2), (4, 2), (6, 1), (7, 1), (8, 1))
NK = 9
Z_ORDER = (0, 1, 7, 2, 6, 3, 5, 4)


def iota(axis, shape=(256, 256)):
    return lax.broadcasted_iota(jnp.int32, shape, axis)


def dot(a, b, ca, cb):
    return lax.dot_general(a, b, (((ca,), (cb,)), ((), ())), preferred_element_type=F32)


def body(
    wt, act, pre, og, out,
    wtmp, W, K, D, Q, XT, up, upsend,
    own1, sb1, rb1, sa, ra, sb, rb, zf, zown, zs, zr,
    s_z, s_yp, s_ym, s_hp, s_hm, s_by, s_bp, s_bm, s_sib, s_x, s_1, s_a, s_b, s_3, r_3,
    r_z, r_yp, r_ym, r_h, r_by, r_bz, r_sib, r_x, r_1, r_a, r_b,
):
    seg = lax.axis_index("segment")
    dp = lax.axis_index("dp")
    y = dp // 16
    z = (dp // 2) % 8
    c = dp % 2

    def at(yy, zz, cc):
        return (seg, yy * 16 + zz * 2 + cc)

    yp = at((y + 1) % NY, z, c)
    ym = at((y + 3) % NY, z, c)
    sib = at(y, z, 1 - c)

    def zpeer(d):
        return at(y, (z + d) % NZ, c)

    def rc(src, dst, ss, rs, dev):
        return pltpu.make_async_remote_copy(
            src_ref=src, dst_ref=dst, send_sem=ss, recv_sem=rs, device_id=dev, device_id_type=MESH
        )

    barrier = pltpu.get_barrier_semaphore()
    peers = [yp, ym, sib] + [zpeer(d) for d in (1, 7, 2, 6)]
    peers += [((seg + 1) % NSEG, dp), ((seg + NSEG - 1) % NSEG, dp)]
    for dev in peers:
        pl.semaphore_signal(barrier, inc=1, device_id=dev, device_id_type=MESH)

    wtmp[104:112, :] = jnp.zeros((8, C), F32)
    for t in range(27):
        wtmp[4 * t : 4 * t + 4, :] = wt[t]
    W[z, c, y] = wtmp[...].astype(BF16)

    Q[:, :, 0] = jnp.zeros((9, MICRO, 32, C), BF16)
    Q[:, :, 5] = jnp.zeros((9, MICRO, 32, C), BF16)

    def derivative(i, carry):
        rows = pl.ds(pl.multiple_of(i * 128, 128), 128)
        p = pre[rows, :].astype(F32)
        sig = jax.nn.sigmoid(p)
        D[rows, :] = sig * (1.0 + p * (1.0 - sig))
        return carry

    row = iota(0)
    ch = (
        ((y + ((row >> 5) & 3)) & 3) * 64
        + ((z + ((row >> 2) & 7)) & 7) * 8
        + ((c + (row >> 7)) & 1) * 4
        + (row & 3)
    )
    pick = jnp.where(iota(1) == ch, 1.0, 0.0).astype(BF16)
    XT[...] = dot(pick, act[...], 1, 1).astype(BF16)
    lax.fori_loop(0, MICRO, derivative, 0)

    pl.semaphore_wait(barrier, len(peers))

    def part(d, yy, rows):
        return W.at[(z + 8 - d) % NZ, c, yy, rows]

    first = pl.ds(0, SPLIT)
    first_a = pl.ds(0, 64)
    first_b = pl.ds(64, 48)
    last = pl.ds(SPLIT, MSG - SPLIT)
    every = pl.ds(0, NY)

    def cp_z(d):
        src, by, rows, sem = Z_HOPS[d]
        piece = part(src, y, (first, first_a, first_b)[rows])
        return rc(piece, piece, s_z.at[sem], r_z.at[d % NZ], zpeer(by))

    def in_z(d):
        piece = part(d, y, first)
        return rc(piece, piece, s_z.at[0], r_z.at[d], zpeer(1))

    def cp_yp(d, src=None):
        piece = part(d, y if src is None else src, first)
        return rc(piece, piece, s_yp, r_yp.at[d], yp)

    def cp_ym(d, src=None):
        piece = part(d, y if src is None else src, first)
        return rc(piece, piece, s_ym, r_ym.at[d], ym)

    def cp_hp(d, src):
        piece = part(d, src, first_a)
        return rc(piece, piece, s_hp, r_h.at[d], yp)

    def cp_hm(d, src):
        piece = part(d, src, first_b)
        return rc(piece, piece, s_hm, r_h.at[d], ym)

    def in_h(d):
        piece = part(d, (y + 2) % NY, first)
        return rc(piece, piece, s_hp, r_h.at[d], yp)

    def cp_by(e):
        piece = part(0, y, last)
        return rc(piece, piece, s_by, r_by.at[e], at((y + e) % NY, z, c))

    def in_by(e):
        piece = part(0, (y + NY - e) % NY, last)
        return rc(piece, piece, s_by, r_by.at[e], yp)

    def cp_bz(d):
        if d == 4:
            piece = part(3, pl.ds(0, 2), last)
        elif d == 0:
            piece = part(5, pl.ds(2, 2), last)
        else:
            piece = part(d - 1 if d < 4 else (d + 1) % NZ, every, last)
        back = d in (1, 2, 3, 4)
        return rc(piece, piece, s_bp if back else s_bm, r_bz.at[d], zpeer(1 if back else 7))

    def in_bz(d):
        if d == 4:
            piece = part(4, pl.ds(0, 2), last)
        elif d == 0:
            piece = part(4, pl.ds(2, 2), last)
        else:
            piece = part(d, every, last)
        return rc(piece, piece, s_bp, r_bz.at[d], zpeer(1))

    def cp_sib(d, cc):
        piece = W.at[(z + 8 - d) % NZ, cc]
        return rc(piece, piece, s_sib, r_sib.at[d], sib)

    up_of = (y + 1) % NY
    down_of = (y + 3) % NY
    for d in (1, 7, 2, 6):
        cp_z(d).start()
    cp_yp(0).start()
    cp_ym(0).start()

    lag = len(Z_ORDER)
    for j in range(lag + 4):
        if 0 < j < lag:
            d = Z_ORDER[j]
            in_z(d).wait_recv()
            for nxt in {1: (3,), 7: (5,), 2: (4,), 6: (12,)}.get(d, ()):
                cp_z(nxt).start()
            cp_yp(d).start()
            cp_ym(d).start()
        if 0 <= j - 2 < lag:
            d = Z_ORDER[j - 2]
            cp_yp(d, down_of).wait_recv()
            cp_hp(d, down_of).start()
            cp_ym(d, up_of).wait_recv()
            cp_hm(d, up_of).start()
        if 0 <= j - 4 < lag:
            d = Z_ORDER[j - 4]
            in_h(d).wait_recv()
            cp_sib(d, c).start()

    r = iota(0)
    src = ((r >> 3) & 1) * 128 + ((r >> 2) & 1) * 64 + ((r >> 4) & 3) * 16 + (r >> 6) * 4 + (r & 3)
    order = jnp.where(iota(1) == src, 1.0, 0.0).astype(BF16)

    def assemble(zp):
        for q in range(7):
            b = W[pl.ds(2 * zp, 2), :, :, 16 * q : 16 * q + 16, :].reshape(256, C)
            m = dot(order, b, 1, 0).astype(BF16)
            for tap in range(4):
                for yy in range(NY):
                    K[4 * q + tap, pl.ds(pl.multiple_of(64 * yy + 16 * zp, 16), 16), :] = m[
                        64 * tap + 16 * yy : 64 * tap + 16 * yy + 16
                    ]

    half_z = z // 2
    for needed, pair in (((0, 1, 7), 0), ((2, 3), 3), ((6, 5), 1), ((4,), 2)):
        for d in needed:
            cp_sib(d, 1 - c).wait_recv()

        @pl.when(seg > 0)
        def _():
            assemble((half_z + pair) % 4)

    @pl.when(jnp.logical_and(seg > 0, seg < NSEG - 1))
    def _():
        same = jnp.where(iota(0) == iota(1), 1.0, 0.0).astype(BF16)

        def turn(t, carry):
            K[t] = dot(same, K[t], 1, 1).astype(BF16)
            return carry

        lax.fori_loop(0, 27, turn, 0)

    def hop(g):
        return rc(upsend.at[g], up.at[g], s_x, r_x.at[g], (jnp.maximum(seg - 1, 0), dp))

    def pipe(g, carry):
        rows = pl.ds(pl.multiple_of(g * RG, RG), RG)

        @pl.when(seg == NSEG - 1)
        def _():
            up[g] = og[rows, :]

        @pl.when(seg < NSEG - 1)
        def _():
            hop(g).wait_recv()

        u = up[g].astype(F32)
        gp = (u * D[rows, :]).astype(BF16).astype(F32)
        cell_y = iota(0, (RG, C)) & 7
        zero = jnp.zeros((4 * G, 8, C), F32)
        for oy in (-1, 0, 1):
            if oy == 1:
                s = jnp.where(cell_y == 0, 0.0, pltpu.roll(gp, 1, 0))
            elif oy == -1:
                s = jnp.where(cell_y == 7, 0.0, pltpu.roll(gp, RG - 1, 0))
            else:
                s = gp
            s = s.reshape(4 * G, 32, C)
            for ox in (-1, 0, 1):
                if ox == 1:
                    v = jnp.concatenate([zero, s[:, :24]], axis=1)
                elif ox == -1:
                    v = jnp.concatenate([s[:, 8:], zero], axis=1)
                else:
                    v = s
                Q[3 * (ox + 1) + oy + 1, pl.ds(G * g, G), 1:5] = v.reshape(G, 4, 32, C).astype(BF16)

        def back(side):
            total = u
            for k in range(NK):
                for a in range(3):
                    q = Q[k, pl.ds(G * g, G), 2 - a : 6 - a].reshape(RG, C)
                    total = total + dot(q, K[9 * a + k], 1, side)
            upsend[g] = total.astype(BF16)
            hop(g).start()

        @pl.when(seg == NSEG - 1)
        def _():
            back(1)

        @pl.when(jnp.logical_and(seg > 0, seg < NSEG - 1))
        def _():
            back(0)

        return carry

    lax.fori_loop(0, NG, pipe, 0)

    def cp_1(k):
        return rc(sb1.at[k], rb1.at[k], s_1, r_1.at[k], sib)

    def cp_a(k, way):
        return rc(sa.at[k, way], ra.at[k, way], s_a, r_a.at[k], (yp, ym)[way])

    def in_a(k):
        return rc(sa.at[k], ra.at[k], s_a, r_a.at[k], yp)

    def cp_b(k, way):
        return rc(sb.at[k, way], rb.at[k, way], s_b, r_b.at[k], (yp, ym)[way])

    def in_b(k):
        return rc(sb.at[k], rb.at[k], s_b, r_b.at[k], yp)

    def cp_3(d, k, n):
        return rc(zs.at[d, pl.ds(k, n)], zr.at[d, pl.ds(k, n)], s_3, r_3, zpeer(d))

    for d in range(NZ):
        zf[d, 8:16, :] = jnp.zeros((8, C), F32)

    def stage_a(k):
        for a in range(3):
            g = dot(XT[...], Q[k, :, 2 - a : 6 - a].reshape(1024, C), 1, 0)
            own1[k, a] = g[:128]
            sb1[k, a] = g[128:].astype(BF16)
        cp_1(k).start()

    def stage_b(k):
        cp_1(k).wait_recv()
        total = own1[k] + rb1[k].astype(F32)
        own1[k] = total
        sa[k, 0] = total[:, 64:96, :128].astype(BF16)
        sa[k, 1] = total[:, 64:96, 128:].astype(BF16)
        cp_a(k, 0).start()
        cp_a(k, 1).start()

    def stage_c(k):
        in_a(k).wait_recv()
        sb[k, 0, :, :, :128] = (own1[k, :, 32:64, :128] + ra[k, 0].astype(F32)).astype(BF16)
        sb[k, 0, :, :, 128:] = own1[k, :, 32:64, 128:].astype(BF16)
        sb[k, 1, :, :, :128] = own1[k, :, 96:128, :128].astype(BF16)
        sb[k, 1, :, :, 128:] = (own1[k, :, 96:128, 128:] + ra[k, 1].astype(F32)).astype(BF16)
        cp_b(k, 0).start()
        cp_b(k, 1).start()

    def stage_d(k):
        in_b(k).wait_recv()
        for a in range(3):
            ys = own1[k, a, 0:32] + rb[k, 0, a].astype(F32) + rb[k, 1, a].astype(F32)
            for d in range(NZ):
                zf[d, 4 * a : 4 * a + 4, :] = ys[4 * d : 4 * d + 4]
        zown[k] = zf[0]
        zs[:, k] = zf[...].astype(BF16)
        for start, n in Z_GROUPS:

            @pl.when(k == start + n - 1)
            def _():
                for d in range(1, NZ):
                    cp_3(d, start, n).start()

    def step(i, carry):
        for lead, stage in ((LAG_D, stage_d), (LAG_C, stage_c), (LAG_B, stage_b), (0, stage_a)):
            k = i - lead

            @pl.when(jnp.logical_and(k >= 0, k < NK))
            def _():
                stage(k)

        return carry

    lax.fori_loop(0, NK + LAG_D, step, 0)

    rc(zs.at[pl.ds(1, NZ - 1)], zr.at[pl.ds(1, NZ - 1)], s_3, r_3, yp).wait_recv()

    def finish(k, carry):
        total = zown[k]
        for d in range(1, NZ):
            total = total + zr[d, k].astype(F32)
        for a in range(3):
            out[9 * a + k] = total[4 * a : 4 * a + 4]
        return carry

    lax.fori_loop(0, NK, finish, 0)

    def sent(ref, sem):
        rc(ref, ref, sem, sem, yp).wait_send()

    sent(W.at[pl.ds(0, 6), c, y, first], s_z.at[0])
    sent(part(4, y, first_a), s_z.at[1])
    sent(part(4, y, first_b), s_z.at[2])
    sent(W.at[:, c, y, first], s_yp)
    sent(W.at[:, c, y, first], s_ym)
    sent(W.at[:, c, y, first_a], s_hp)
    sent(W.at[:, c, y, first_b], s_hm)
    sent(W.at[:, c], s_sib)

    @pl.when(seg > 0)
    def _():
        sent(upsend, s_x)

    sent(sb1, s_1)
    sent(sa, s_a)
    sent(sb, s_b)
    sent(zs.at[pl.ds(1, NZ - 1)], s_3)


def gradient(wt, act, pre, og):
    vmem = pltpu.VMEM
    dma = pltpu.SemaphoreType.DMA
    scratch = [
        vmem((MSG, C), F32),
        vmem((NZ, 2, NY, MSG, C), BF16),
        vmem((28, C, C), BF16),
        vmem((MICRO * 128, C), F32),
        vmem((9, MICRO, 6, 32, C), BF16),
        vmem((C, MICRO * 128), BF16),
        vmem((NG, RG, C), BF16),
        vmem((NG, RG, C), BF16),
        vmem((NK, 3, 128, C), F32),
        vmem((NK, 3, 128, C), BF16),
        vmem((NK, 3, 128, C), BF16),
    ]
    scratch += [vmem((NK, 2, 3, 32, 128), BF16)] * 2
    scratch += [vmem((NK, 2, 3, 32, C), BF16)] * 2
    scratch += [
        vmem((NZ, 16, C), F32),
        vmem((NK, 16, C), F32),
        vmem((NZ, NK, 16, C), BF16),
        vmem((NZ, NK, 16, C), BF16),
    ]
    scratch += [dma((3,))] + [dma] * 14
    scratch += [dma((NZ,))] * 4 + [dma((NY,))] + [dma((NZ,))] * 2 + [dma((NG,))] + [dma((NK,))] * 3
    return pl.pallas_call(
        body,
        out_shape=jax.ShapeDtypeStruct((27, ROWS, C), F32),
        in_specs=[pl.BlockSpec(memory_space=pltpu.VMEM)] * 4,
        out_specs=pl.BlockSpec(memory_space=pltpu.VMEM),
        scratch_shapes=scratch,
        compiler_params=pltpu.CompilerParams(
            collective_id=0, has_side_effects=True, vmem_limit_bytes=56 << 20
        ),
    )(wt, act, pre, og)


def shards(activations, preacts, out_grad, weights, momentum, noise):
    cells = MICRO * 128
    grads = gradient(
        weights[0].transpose(1, 0, 2),
        activations.reshape(cells, C),
        preacts.reshape(cells, C),
        out_grad.reshape(cells, C),
    ).transpose(1, 0, 2)
    rate = 1.0 / math.sqrt(lax.axis_size("dp") * cells)
    updated = 0.9 * momentum[0] - rate * grads + 0.3 * noise[0]
    return updated[None]


def solution(mesh):
    placed = (
        P("segment", "dp", None, None, None, None),
        P("segment", "dp", None, None, None, None),
        P("dp", None, None, None, None),
        P("segment", "dp", None, None),
        P("segment", "dp", None, None),
        P("segment", "dp", None, None),
    )
    return jax.shard_map(
        shards,
        mesh=mesh,
        in_specs=placed,
        out_specs=P("segment", "dp", None, None),
        check_vma=False,
    )
```

```python
import functools
import math

import jax
import jax.numpy as jnp
from jax import lax
from jax.experimental import pallas as pl
from jax.experimental.pallas import tpu as pltpu
from jax.sharding import PartitionSpec as P

MESH = pl.DeviceIdType.MESH
F32 = jnp.float32
BF16 = jnp.bfloat16

NSEG = 4
NY = 4
NZ = 8
C = 256
ROWS = 4
MICRO = 8
G = 1
NG = MICRO // G
RATE = 1.0 / math.sqrt(NY * NZ * 2 * MICRO * 128)
RG = G * 128
MSG = 112
Z_HOPS = {
    1: (0, 1, 0, 0), 7: (0, 7, 0, 0), 2: (0, 2, 0, 0), 6: (0, 6, 0, 0), 3: (1, 2, 0, 0), 5: (7, 6, 0, 0),
    4: (2, 2, 1, 1), 12: (6, 6, 2, 2),
}
BLAG = 2
SPLIT = 96
LAG_B, LAG_C, LAG_D = 2, 5, 9

Z_GROUPS = ((0, 2), (2, 2), (4, 2), (6, 1), (7, 1), (8, 1))
NK = 9
Z_ORDER = (0, 1, 7, 2, 6, 3, 5, 4)


def iota(axis, shape=(256, 256)):
    return lax.broadcasted_iota(jnp.int32, shape, axis)


def dot(a, b, ca, cb):
    return lax.dot_general(a, b, (((ca,), (cb,)), ((), ())), preferred_element_type=F32)


def body(
    wt, mom_in, noise_in, act_in, pre_in, og_in, out,
    mom, noise, act, pre, og, s_in,
    wtmp, W, K, D, Q, XT, up, upsend,
    own1, sb1, rb1, sa, ra, sb, rb, zf, zown, zs, zr,
    s_z, s_yp, s_ym, s_hp, s_hm, s_by, s_bp, s_bm, s_sib, s_x, s_1, s_a, s_b, s_3, r_3,
    r_z, r_yp, r_ym, r_h, r_by, r_bz, r_sib, r_x, r_1, r_a, r_b,
):
    seg = lax.axis_index("segment")
    dp = lax.axis_index("dp")
    y = dp // 16
    z = (dp // 2) % 8
    c = dp % 2

    def at(yy, zz, cc):
        return (seg, yy * 16 + zz * 2 + cc)

    yp = at((y + 1) % NY, z, c)
    ym = at((y + 3) % NY, z, c)
    sib = at(y, z, 1 - c)

    def zpeer(d):
        return at(y, (z + d) % NZ, c)

    def rc(src, dst, ss, rs, dev):
        return pltpu.make_async_remote_copy(
            src_ref=src, dst_ref=dst, send_sem=ss, recv_sem=rs, device_id=dev, device_id_type=MESH
        )

    fetches = [
        pltpu.make_async_copy(src, dst, s_in.at[n])
        for n, (src, dst) in enumerate(
            ((pre_in, pre), (act_in, act), (og_in, og), (mom_in, mom), (noise_in, noise))
        )
    ]
    for fetch in fetches:
        fetch.start()

    barrier = pltpu.get_barrier_semaphore()
    peers = [yp, ym, at((y + 2) % NY, z, c), sib] + [zpeer(d) for d in (1, 7, 2, 6)]
    peers += [((seg + 1) % NSEG, dp), ((seg + NSEG - 1) % NSEG, dp)]
    for dev in peers:
        pl.semaphore_signal(barrier, inc=1, device_id=dev, device_id_type=MESH)

    wtmp[104:112, :] = jnp.zeros((8, C), F32)
    for t in range(27):
        wtmp[4 * t : 4 * t + 4, :] = wt[t]
    W[z, c, y] = wtmp[...].astype(BF16)

    for fetch in fetches:
        fetch.wait()

    Q[:, :, 0] = jnp.zeros((9, MICRO, 32, C), BF16)
    Q[:, :, 5] = jnp.zeros((9, MICRO, 32, C), BF16)

    def derivative(i, carry):
        rows = pl.ds(pl.multiple_of(i * 128, 128), 128)
        p = pre[rows, :].astype(F32)
        sig = jax.nn.sigmoid(p)
        D[rows, :] = sig * (1.0 + p * (1.0 - sig))
        return carry

    row = iota(0)
    ch = (
        ((y + ((row >> 5) & 3)) & 3) * 64
        + ((z + ((row >> 2) & 7)) & 7) * 8
        + ((c + (row >> 7)) & 1) * 4
        + (row & 3)
    )
    pick = jnp.where(iota(1) == ch, 1.0, 0.0).astype(BF16)
    XT[...] = dot(pick, act[...], 1, 1).astype(BF16)
    lax.fori_loop(0, MICRO, derivative, 0)

    pl.semaphore_wait(barrier, len(peers))

    def part(d, yy, rows):
        return W.at[(z + 8 - d) % NZ, c, yy, rows]

    first = pl.ds(0, SPLIT)
    first_a = pl.ds(0, SPLIT // 2)
    first_b = pl.ds(SPLIT // 2, SPLIT // 2)
    last = pl.ds(SPLIT, MSG - SPLIT)
    every = pl.ds(0, NY)

    def cp_z(d):
        src, by, rows, sem = Z_HOPS[d]
        piece = part(src, y, (first, first_a, first_b)[rows])
        return rc(piece, piece, s_z.at[sem], r_z.at[d % NZ], zpeer(by))

    def in_z(d):
        piece = part(d, y, first)
        return rc(piece, piece, s_z.at[0], r_z.at[d], zpeer(1))

    def cp_yp(d, src=None):
        piece = part(d, y if src is None else src, first)
        return rc(piece, piece, s_yp, r_yp.at[d], yp)

    def cp_ym(d, src=None):
        piece = part(d, y if src is None else src, first)
        return rc(piece, piece, s_ym, r_ym.at[d], ym)

    def cp_hp(d, src):
        piece = part(d, src, first_a)
        return rc(piece, piece, s_hp, r_h.at[d], yp)

    def cp_hm(d, src):
        piece = part(d, src, first_b)
        return rc(piece, piece, s_hm, r_h.at[d], ym)

    def in_h(d):
        piece = part(d, (y + 2) % NY, first)
        return rc(piece, piece, s_hp, r_h.at[d], yp)

    def cp_by(e):
        piece = part(0, y, last)
        return rc(piece, piece, s_by, r_by.at[e], at((y + e) % NY, z, c))

    def in_by(e):
        piece = part(0, (y + NY - e) % NY, last)
        return rc(piece, piece, s_by, r_by.at[e], yp)

    def cp_bz(d):
        src, by, rows, sem = Z_HOPS[d]
        piece = part(src, (every, pl.ds(0, 2), pl.ds(2, 2))[rows], last)
        return rc(piece, piece, s_bm if sem else s_bp, r_bz.at[d % 12], zpeer(by))

    def in_bz(d):
        if d == 4:
            piece = part(4, pl.ds(0, 2), last)
        elif d == 0:
            piece = part(4, pl.ds(2, 2), last)
        else:
            piece = part(d, every, last)
        return rc(piece, piece, s_bp, r_bz.at[d], zpeer(1))

    def cp_sib(d, cc):
        piece = W.at[(z + 8 - d) % NZ, cc]
        return rc(piece, piece, s_sib, r_sib.at[d], sib)

    up_of = (y + 1) % NY
    down_of = (y + 3) % NY
    for d in (1, 7, 2, 6):
        cp_z(d).start()
    cp_yp(0).start()
    cp_ym(0).start()
    for e in (1, 3, 2):
        cp_by(e).start()

    lag = len(Z_ORDER)
    for j in range(lag + 4):
        if 0 < j < lag:
            d = Z_ORDER[j]
            in_z(d).wait_recv()
            for nxt in {1: (3,), 7: (5,), 2: (4,), 6: (12,)}.get(d, ()):
                cp_z(nxt).start()
            cp_yp(d).start()
            cp_ym(d).start()
        if 0 <= j - BLAG < lag:
            d = Z_ORDER[j - BLAG]
            if d == 0:
                for e in (1, 3, 2):
                    in_by(e).wait_recv()
                for nxt in (1, 7, 2, 6):
                    cp_bz(nxt).start()
            elif d == 4:
                in_bz(4).wait_recv()
                in_bz(0).wait_recv()
            else:
                in_bz(d).wait_recv()
                for nxt in {1: (3,), 7: (5,), 2: (4,), 6: (12,)}.get(d, ()):
                    cp_bz(nxt).start()
        if 0 <= j - 2 < lag:
            d = Z_ORDER[j - 2]
            cp_yp(d, down_of).wait_recv()
            cp_hp(d, down_of).start()
            cp_ym(d, up_of).wait_recv()
            cp_hm(d, up_of).start()
        if 0 <= j - 4 < lag:
            d = Z_ORDER[j - 4]
            in_h(d).wait_recv()
            cp_sib(d, c).start()

    r = iota(0)
    src = ((r >> 3) & 1) * 128 + ((r >> 2) & 1) * 64 + ((r >> 4) & 3) * 16 + (r >> 6) * 4 + (r & 3)
    order = jnp.where(iota(1) == src, 1.0, 0.0).astype(BF16)

    def assemble(zp):
        for q in range(7):
            b = W[pl.ds(2 * zp, 2), :, :, 16 * q : 16 * q + 16, :].reshape(256, C)
            m = dot(order, b, 1, 0).astype(BF16)
            for tap in range(4):
                for yy in range(NY):
                    K[4 * q + tap, pl.ds(pl.multiple_of(64 * yy + 16 * zp, 16), 16), :] = m[
                        64 * tap + 16 * yy : 64 * tap + 16 * yy + 16
                    ]

    half_z = z // 2
    for needed, pair in (((0, 1, 7), 0), ((2, 3), 3), ((6, 5), 1), ((4,), 2)):
        for d in needed:
            cp_sib(d, 1 - c).wait_recv()

        @pl.when(seg > 0)
        def _():
            assemble((half_z + pair) % 4)

    @pl.when(jnp.logical_and(seg > 0, seg < NSEG - 1))
    def _():
        same = jnp.where(iota(0) == iota(1), 1.0, 0.0).astype(BF16)

        def turn(t, carry):
            K[t] = dot(same, K[t], 1, 1).astype(BF16)
            return carry

        lax.fori_loop(0, 27, turn, 0)

    def hop(g):
        return rc(upsend.at[g], up.at[g], s_x, r_x.at[g], (jnp.maximum(seg - 1, 0), dp))

    def pipe(g, carry):
        rows = pl.ds(pl.multiple_of(g * RG, RG), RG)

        @pl.when(seg == NSEG - 1)
        def _():
            up[g] = og[rows, :]

        @pl.when(seg < NSEG - 1)
        def _():
            hop(g).wait_recv()

        u = up[g].astype(F32)
        gp = (u * D[rows, :]).astype(BF16).astype(F32)
        cell_y = iota(0, (RG, C)) & 7
        zero = jnp.zeros((4 * G, 8, C), F32)
        for oy in (-1, 0, 1):
            if oy == 1:
                s = jnp.where(cell_y == 0, 0.0, pltpu.roll(gp, 1, 0))
            elif oy == -1:
                s = jnp.where(cell_y == 7, 0.0, pltpu.roll(gp, RG - 1, 0))
            else:
                s = gp
            s = s.reshape(4 * G, 32, C)
            for ox in (-1, 0, 1):
                if ox == 1:
                    v = jnp.concatenate([zero, s[:, :24]], axis=1)
                elif ox == -1:
                    v = jnp.concatenate([s[:, 8:], zero], axis=1)
                else:
                    v = s
                Q[3 * (ox + 1) + oy + 1, pl.ds(G * g, G), 1:5] = v.reshape(G, 4, 32, C).astype(BF16)

        def back(side):
            total = u
            for k in range(NK):
                for a in range(3):
                    q = Q[k, pl.ds(G * g, G), 2 - a : 6 - a].reshape(RG, C)
                    total = total + dot(q, K[9 * a + k], 1, side)
            upsend[g] = total.astype(BF16)
            hop(g).start()

        @pl.when(seg == NSEG - 1)
        def _():
            back(1)

        @pl.when(jnp.logical_and(seg > 0, seg < NSEG - 1))
        def _():
            back(0)

        return carry

    lax.fori_loop(0, NG, pipe, 0)

    def cp_1(k):
        return rc(sb1.at[k], rb1.at[k], s_1, r_1.at[k], sib)

    def cp_a(k, way):
        return rc(sa.at[k, way], ra.at[k, way], s_a, r_a.at[k], (yp, ym)[way])

    def in_a(k):
        return rc(sa.at[k], ra.at[k], s_a, r_a.at[k], yp)

    def cp_b(k, way):
        return rc(sb.at[k, way], rb.at[k, way], s_b, r_b.at[k], (yp, ym)[way])

    def in_b(k):
        return rc(sb.at[k], rb.at[k], s_b, r_b.at[k], yp)

    def cp_3(d, k, n):
        return rc(zs.at[d, pl.ds(k, n)], zr.at[d, pl.ds(k, n)], s_3, r_3, zpeer(d))

    for d in range(NZ):
        zf[d, 8:16, :] = jnp.zeros((8, C), F32)

    def stage_a(k):
        for a in range(3):
            g = dot(XT[...], Q[k, :, 2 - a : 6 - a].reshape(1024, C), 1, 0)
            own1[k, a] = g[:128]
            sb1[k, a] = g[128:].astype(BF16)
        cp_1(k).start()

    def stage_b(k):
        cp_1(k).wait_recv()
        total = own1[k] + rb1[k].astype(F32)
        own1[k] = total
        sa[k, 0] = total[:, 64:96, :128].astype(BF16)
        sa[k, 1] = total[:, 64:96, 128:].astype(BF16)
        cp_a(k, 0).start()
        cp_a(k, 1).start()

    def stage_c(k):
        in_a(k).wait_recv()
        sb[k, 0, :, :, :128] = (own1[k, :, 32:64, :128] + ra[k, 0].astype(F32)).astype(BF16)
        sb[k, 0, :, :, 128:] = own1[k, :, 32:64, 128:].astype(BF16)
        sb[k, 1, :, :, :128] = own1[k, :, 96:128, :128].astype(BF16)
        sb[k, 1, :, :, 128:] = (own1[k, :, 96:128, 128:] + ra[k, 1].astype(F32)).astype(BF16)
        cp_b(k, 0).start()
        cp_b(k, 1).start()

    def stage_d(k):
        in_b(k).wait_recv()
        for a in range(3):
            ys = own1[k, a, 0:32] + rb[k, 0, a].astype(F32) + rb[k, 1, a].astype(F32)
            for d in range(NZ):
                zf[d, 4 * a : 4 * a + 4, :] = ys[4 * d : 4 * d + 4]
        zown[k] = zf[0]
        zs[:, k] = zf[...].astype(BF16)
        for start, n in Z_GROUPS:

            @pl.when(k == start + n - 1)
            def _():
                for d in range(1, NZ):
                    cp_3(d, start, n).start()

    def step(i, carry):
        for lead, stage in ((LAG_D, stage_d), (LAG_C, stage_c), (LAG_B, stage_b), (0, stage_a)):
            k = i - lead

            @pl.when(jnp.logical_and(k >= 0, k < NK))
            def _():
                stage(k)

        return carry

    lax.fori_loop(0, NK + LAG_D, step, 0)

    rc(zs.at[pl.ds(1, NZ - 1)], zr.at[pl.ds(1, NZ - 1)], s_3, r_3, yp).wait_recv()

    def finish(k, carry):
        total = zown[k]
        for d in range(1, NZ):
            total = total + zr[d, k].astype(F32)
        for a in range(3):
            t = 9 * a + k
            out[t] = 0.9 * mom[t] - RATE * total[4 * a : 4 * a + 4] + 0.3 * noise[t]
        return carry

    lax.fori_loop(0, NK, finish, 0)

    def sent(ref, sem):
        rc(ref, ref, sem, sem, yp).wait_send()

    sent(W.at[pl.ds(0, 6), c, y, first], s_z.at[0])
    sent(part(4, y, first_a), s_z.at[1])
    sent(part(4, y, first_b), s_z.at[2])
    sent(W.at[:, c, y, first], s_yp)
    sent(W.at[:, c, y, first], s_ym)
    sent(W.at[:, c, y, first_a], s_hp)
    sent(W.at[:, c, y, first_b], s_hm)
    sent(W.at[0, c, pl.ds(0, 3), last], s_by)
    sent(W.at[pl.ds(0, 6), c, every, last], s_bp)
    sent(part(4, every, last), s_bm)
    sent(W.at[:, c], s_sib)

    @pl.when(seg > 0)
    def _():
        sent(upsend, s_x)

    sent(sb1, s_1)
    sent(sa, s_a)
    sent(sb, s_b)
    sent(zs.at[pl.ds(1, NZ - 1)], s_3)


def momentum_step(wt, mom, noise, act, pre, og):
    vmem = pltpu.VMEM
    dma = pltpu.SemaphoreType.DMA
    scratch = [
        vmem((27, ROWS, C), F32),
        vmem((27, ROWS, C), F32),
        vmem((MICRO * 128, C), BF16),
        vmem((MICRO * 128, C), BF16),
        vmem((MICRO * 128, C), BF16),
        dma((5,)),
        vmem((MSG, C), F32),
        vmem((NZ, 2, NY, MSG, C), BF16),
        vmem((28, C, C), BF16),
        vmem((MICRO * 128, C), F32),
        vmem((9, MICRO, 6, 32, C), BF16),
        vmem((C, MICRO * 128), BF16),
        vmem((NG, RG, C), BF16),
        vmem((NG, RG, C), BF16),
        vmem((NK, 3, 128, C), F32),
        vmem((NK, 3, 128, C), BF16),
        vmem((NK, 3, 128, C), BF16),
    ]
    scratch += [vmem((NK, 2, 3, 32, 128), BF16)] * 2
    scratch += [vmem((NK, 2, 3, 32, C), BF16)] * 2
    scratch += [
        vmem((NZ, 16, C), F32),
        vmem((NK, 16, C), F32),
        vmem((NZ, NK, 16, C), BF16),
        vmem((NZ, NK, 16, C), BF16),
    ]
    scratch += [dma((3,))] + [dma] * 14
    scratch += [dma((NZ,))] * 4 + [dma((NY,))] + [dma((NZ,))] * 2 + [dma((NG,))] + [dma((NK,))] * 3
    return pl.pallas_call(
        body,
        out_shape=jax.ShapeDtypeStruct((27, ROWS, C), F32),
        in_specs=[pl.BlockSpec(memory_space=pltpu.VMEM)] + [pl.BlockSpec(memory_space=pl.ANY)] * 5,
        out_specs=pl.BlockSpec(memory_space=pltpu.VMEM),
        scratch_shapes=scratch,
        compiler_params=pltpu.CompilerParams(
            collective_id=0, has_side_effects=True, vmem_limit_bytes=56 << 20
        ),
    )(wt, mom, noise, act, pre, og)


def shards(activations, preacts, out_grad, weights, momentum, noise):
    cells = MICRO * 128
    updated = momentum_step(
        weights[0].transpose(1, 0, 2),
        momentum[0].transpose(1, 0, 2),
        noise[0].transpose(1, 0, 2),
        activations.reshape(cells, C),
        preacts.reshape(cells, C),
        out_grad.reshape(cells, C),
    )
    return updated.transpose(1, 0, 2)[None]


def solution(mesh):
    placed = (
        P("segment", "dp", None, None, None, None),
        P("segment", "dp", None, None, None, None),
        P("dp", None, None, None, None),
        P("segment", "dp", None, None),
        P("segment", "dp", None, None),
        P("segment", "dp", None, None),
    )
    return jax.shard_map(
        shards,
        mesh=mesh,
        in_specs=placed,
        out_specs=P("segment", "dp", None, None),
        check_vma=False,
    )
```

```python
import functools
import math

import jax
import jax.numpy as jnp
from jax import lax
from jax.experimental import pallas as pl
from jax.experimental.pallas import tpu as pltpu
from jax.sharding import PartitionSpec as P

MESH = pl.DeviceIdType.MESH
F32 = jnp.float32
BF16 = jnp.bfloat16

NSEG = 4
NY = 4
NZ = 8
C = 256
ROWS = 4
MICRO = 8
G = 1
NG = MICRO // G
RATE = 1.0 / math.sqrt(NY * NZ * 2 * MICRO * 128)
RG = G * 128
MSG = 112
Z_HOPS = {
    1: (0, 1, 0, 0), 7: (0, 7, 0, 0), 2: (0, 2, 0, 0), 6: (0, 6, 0, 0), 3: (1, 2, 0, 0), 5: (7, 6, 0, 0),
    4: (2, 2, 1, 1), 12: (6, 6, 2, 2),
}
BLAG = 2
SPLIT = 96
LAG_B, LAG_C, LAG_D = 4, 8, 12

Z_GROUPS = ((0, 2), (2, 2), (4, 2), (6, 1), (7, 1), (8, 1))
NK = 9
Z_ORDER = (0, 1, 7, 2, 6, 3, 5, 4)


def iota(axis, shape=(256, 256)):
    return lax.broadcasted_iota(jnp.int32, shape, axis)


def dot(a, b, ca, cb):
    return lax.dot_general(a, b, (((ca,), (cb,)), ((), ())), preferred_element_type=F32)


def body(
    wt, mom_in, noise_in, act_in, pre_in, og_in, out,
    mom, noise, act, pre, og, s_in,
    wtmp, W, K, D, Q, XT, up, upsend,
    own1, sb1, rb1, sa, ra, sb, rb, zf, zown, zs, zr,
    s_z, s_yp, s_ym, s_hp, s_hm, s_by, s_bp, s_bm, s_sib, s_x, s_1, s_a, s_b, s_3, r_3,
    r_z, r_yp, r_ym, r_h, r_by, r_bz, r_sib, r_x, r_1, r_a, r_b,
):
    seg = lax.axis_index("segment")
    dp = lax.axis_index("dp")
    y = dp // 16
    z = (dp // 2) % 8
    c = dp % 2

    def at(yy, zz, cc):
        return (seg, yy * 16 + zz * 2 + cc)

    yp = at((y + 1) % NY, z, c)
    ym = at((y + 3) % NY, z, c)
    sib = at(y, z, 1 - c)

    def zpeer(d):
        return at(y, (z + d) % NZ, c)

    def rc(src, dst, ss, rs, dev):
        return pltpu.make_async_remote_copy(
            src_ref=src, dst_ref=dst, send_sem=ss, recv_sem=rs, device_id=dev, device_id_type=MESH
        )

    fetches = [
        pltpu.make_async_copy(src, dst, s_in.at[n])
        for n, (src, dst) in enumerate(
            ((pre_in, pre), (act_in, act), (og_in, og), (mom_in, mom), (noise_in, noise))
        )
    ]
    for fetch in fetches:
        fetch.start()

    barrier = pltpu.get_barrier_semaphore()
    peers = [yp, ym, at((y + 2) % NY, z, c), sib] + [zpeer(d) for d in (1, 7, 2, 6)]
    peers += [((seg + 1) % NSEG, dp), ((seg + NSEG - 1) % NSEG, dp)]
    for dev in peers:
        pl.semaphore_signal(barrier, inc=1, device_id=dev, device_id_type=MESH)

    wtmp[104:112, :] = jnp.zeros((8, C), F32)
    for t in range(27):
        wtmp[4 * t : 4 * t + 4, :] = wt[t]
    W[z, c, y] = wtmp[...].astype(BF16)

    for fetch in fetches:
        fetch.wait()

    Q[:, :, 0] = jnp.zeros((9, MICRO, 32, C), BF16)
    Q[:, :, 5] = jnp.zeros((9, MICRO, 32, C), BF16)

    def derivative(i, carry):
        rows = pl.ds(pl.multiple_of(i * 128, 128), 128)
        p = pre[rows, :].astype(F32)
        sig = jax.nn.sigmoid(p)
        D[rows, :] = sig * (1.0 + p * (1.0 - sig))
        return carry

    row = iota(0)
    ch = (
        ((y + ((row >> 5) & 3)) & 3) * 64
        + ((z + ((row >> 2) & 7)) & 7) * 8
        + ((c + (row >> 7)) & 1) * 4
        + (row & 3)
    )
    pick = jnp.where(iota(1) == ch, 1.0, 0.0).astype(BF16)
    XT[...] = dot(pick, act[...], 1, 1).astype(BF16)
    lax.fori_loop(0, MICRO, derivative, 0)

    pl.semaphore_wait(barrier, len(peers))

    def part(d, yy, rows):
        return W.at[(z + 8 - d) % NZ, c, yy, rows]

    first = pl.ds(0, SPLIT)
    first_a = pl.ds(0, SPLIT // 2)
    first_b = pl.ds(SPLIT // 2, SPLIT // 2)
    last = pl.ds(SPLIT, MSG - SPLIT)
    every = pl.ds(0, NY)

    def cp_z(d):
        src, by, rows, sem = Z_HOPS[d]
        piece = part(src, y, (first, first_a, first_b)[rows])
        return rc(piece, piece, s_z.at[sem], r_z.at[d % NZ], zpeer(by))

    def in_z(d):
        piece = part(d, y, first)
        return rc(piece, piece, s_z.at[0], r_z.at[d], zpeer(1))

    def cp_yp(d, src=None):
        piece = part(d, y if src is None else src, first)
        return rc(piece, piece, s_yp, r_yp.at[d], yp)

    def cp_ym(d, src=None):
        piece = part(d, y if src is None else src, first)
        return rc(piece, piece, s_ym, r_ym.at[d], ym)

    def cp_hp(d, src):
        piece = part(d, src, first_a)
        return rc(piece, piece, s_hp, r_h.at[d], yp)

    def cp_hm(d, src):
        piece = part(d, src, first_b)
        return rc(piece, piece, s_hm, r_h.at[d], ym)

    def in_h(d):
        piece = part(d, (y + 2) % NY, first)
        return rc(piece, piece, s_hp, r_h.at[d], yp)

    def cp_by(e):
        piece = part(0, y, last)
        return rc(piece, piece, s_by, r_by.at[e], at((y + e) % NY, z, c))

    def in_by(e):
        piece = part(0, (y + NY - e) % NY, last)
        return rc(piece, piece, s_by, r_by.at[e], yp)

    def cp_bz(d):
        src, by, rows, sem = Z_HOPS[d]
        piece = part(src, (every, pl.ds(0, 2), pl.ds(2, 2))[rows], last)
        return rc(piece, piece, s_bm if sem else s_bp, r_bz.at[d % 12], zpeer(by))

    def in_bz(d):
        if d == 4:
            piece = part(4, pl.ds(0, 2), last)
        elif d == 0:
            piece = part(4, pl.ds(2, 2), last)
        else:
            piece = part(d, every, last)
        return rc(piece, piece, s_bp, r_bz.at[d], zpeer(1))

    def cp_sib(d, cc):
        piece = W.at[(z + 8 - d) % NZ, cc]
        return rc(piece, piece, s_sib, r_sib.at[d], sib)

    up_of = (y + 1) % NY
    down_of = (y + 3) % NY
    for d in (1, 7, 2, 6):
        cp_z(d).start()
    cp_yp(0).start()
    cp_ym(0).start()
    for e in (1, 3, 2):
        cp_by(e).start()

    lag = len(Z_ORDER)
    for j in range(lag + 4):
        if 0 < j < lag:
            d = Z_ORDER[j]
            in_z(d).wait_recv()
            for nxt in {1: (3,), 7: (5,), 2: (4,), 6: (12,)}.get(d, ()):
                cp_z(nxt).start()
            cp_yp(d).start()
            cp_ym(d).start()
        if 0 <= j - BLAG < lag:
            d = Z_ORDER[j - BLAG]
            if d == 0:
                for e in (1, 3, 2):
                    in_by(e).wait_recv()
                for nxt in (1, 7, 2, 6):
                    cp_bz(nxt).start()
            elif d == 4:
                in_bz(4).wait_recv()
                in_bz(0).wait_recv()
            else:
                in_bz(d).wait_recv()
                for nxt in {1: (3,), 7: (5,), 2: (4,), 6: (12,)}.get(d, ()):
                    cp_bz(nxt).start()
        if 0 <= j - 2 < lag:
            d = Z_ORDER[j - 2]
            cp_yp(d, down_of).wait_recv()
            cp_hp(d, down_of).start()
            cp_ym(d, up_of).wait_recv()
            cp_hm(d, up_of).start()
        if 0 <= j - 4 < lag:
            d = Z_ORDER[j - 4]
            in_h(d).wait_recv()
            cp_sib(d, c).start()

    r = iota(0)
    src = ((r >> 3) & 1) * 128 + ((r >> 2) & 1) * 64 + ((r >> 4) & 3) * 16 + (r >> 6) * 4 + (r & 3)
    order = jnp.where(iota(1) == src, 1.0, 0.0).astype(BF16)

    def assemble(zp):
        for q in range(7):
            b = W[pl.ds(2 * zp, 2), :, :, 16 * q : 16 * q + 16, :].reshape(256, C)
            m = dot(order, b, 1, 0).astype(BF16)
            for tap in range(4):
                for yy in range(NY):
                    K[4 * q + tap, pl.ds(pl.multiple_of(64 * yy + 16 * zp, 16), 16), :] = m[
                        64 * tap + 16 * yy : 64 * tap + 16 * yy + 16
                    ]

    half_z = z // 2
    for needed, pair in (((0, 1, 7), 0), ((2, 3), 3), ((6, 5), 1), ((4,), 2)):
        for d in needed:
            cp_sib(d, 1 - c).wait_recv()

        @pl.when(seg > 0)
        def _():
            assemble((half_z + pair) % 4)

    @pl.when(jnp.logical_and(seg > 0, seg < NSEG - 1))
    def _():
        same = jnp.where(iota(0) == iota(1), 1.0, 0.0).astype(BF16)

        def turn(t, carry):
            K[t] = dot(same, K[t], 1, 1).astype(BF16)
            return carry

        lax.fori_loop(0, 27, turn, 0)

    def hop(g):
        return rc(upsend.at[g], up.at[g], s_x, r_x.at[g], (jnp.maximum(seg - 1, 0), dp))

    def pipe(g, carry):
        rows = pl.ds(pl.multiple_of(g * RG, RG), RG)

        @pl.when(seg == NSEG - 1)
        def _():
            up[g] = og[rows, :]

        @pl.when(seg < NSEG - 1)
        def _():
            hop(g).wait_recv()

        u = up[g].astype(F32)
        gp = (u * D[rows, :]).astype(BF16).astype(F32)
        cell_y = iota(0, (RG, C)) & 7
        zero = jnp.zeros((4 * G, 8, C), F32)
        for oy in (-1, 0, 1):
            if oy == 1:
                s = jnp.where(cell_y == 0, 0.0, pltpu.roll(gp, 1, 0))
            elif oy == -1:
                s = jnp.where(cell_y == 7, 0.0, pltpu.roll(gp, RG - 1, 0))
            else:
                s = gp
            s = s.reshape(4 * G, 32, C)
            for ox in (-1, 0, 1):
                if ox == 1:
                    v = jnp.concatenate([zero, s[:, :24]], axis=1)
                elif ox == -1:
                    v = jnp.concatenate([s[:, 8:], zero], axis=1)
                else:
                    v = s
                Q[3 * (ox + 1) + oy + 1, pl.ds(G * g, G), 1:5] = v.reshape(G, 4, 32, C).astype(BF16)

        def back(side):
            total = u
            for k in range(NK):
                for a in range(3):
                    q = Q[k, pl.ds(G * g, G), 2 - a : 6 - a].reshape(RG, C)
                    total = total + dot(q, K[9 * a + k], 1, side)
            upsend[g] = total.astype(BF16)
            hop(g).start()

        @pl.when(seg == NSEG - 1)
        def _():
            back(1)

        @pl.when(jnp.logical_and(seg > 0, seg < NSEG - 1))
        def _():
            back(0)

        return carry

    lax.fori_loop(0, NG, pipe, 0)

    def cp_1(k):
        return rc(sb1.at[k], rb1.at[k], s_1, r_1.at[k], sib)

    def cp_a(k, way):
        return rc(sa.at[k, way], ra.at[k, way], s_a, r_a.at[k], (yp, ym)[way])

    def in_a(k):
        return rc(sa.at[k], ra.at[k], s_a, r_a.at[k], yp)

    def cp_b(k, way):
        return rc(sb.at[k, way], rb.at[k, way], s_b, r_b.at[k], (yp, ym)[way])

    def in_b(k):
        return rc(sb.at[k], rb.at[k], s_b, r_b.at[k], yp)

    def cp_3(d, k, n):
        return rc(zs.at[d, pl.ds(k, n)], zr.at[d, pl.ds(k, n)], s_3, r_3, zpeer(d))

    for d in range(NZ):
        zf[d, 8:16, :] = jnp.zeros((8, C), F32)

    def stage_a(k):
        for a in range(3):
            g = dot(XT[...], Q[k, :, 2 - a : 6 - a].reshape(1024, C), 1, 0)
            own1[k, a] = g[:128]
            sb1[k, a] = g[128:].astype(BF16)
        cp_1(k).start()

    def stage_b(k):
        cp_1(k).wait_recv()
        total = own1[k] + rb1[k].astype(F32)
        own1[k] = total
        sa[k, 0] = total[:, 64:96, :128].astype(BF16)
        sa[k, 1] = total[:, 64:96, 128:].astype(BF16)
        cp_a(k, 0).start()
        cp_a(k, 1).start()

    def stage_c(k):
        in_a(k).wait_recv()
        sb[k, 0, :, :, :128] = (own1[k, :, 32:64, :128] + ra[k, 0].astype(F32)).astype(BF16)
        sb[k, 0, :, :, 128:] = own1[k, :, 32:64, 128:].astype(BF16)
        sb[k, 1, :, :, :128] = own1[k, :, 96:128, :128].astype(BF16)
        sb[k, 1, :, :, 128:] = (own1[k, :, 96:128, 128:] + ra[k, 1].astype(F32)).astype(BF16)
        cp_b(k, 0).start()
        cp_b(k, 1).start()

    def stage_d(k):
        in_b(k).wait_recv()
        for a in range(3):
            ys = own1[k, a, 0:32] + rb[k, 0, a].astype(F32) + rb[k, 1, a].astype(F32)
            for d in range(NZ):
                zf[d, 4 * a : 4 * a + 4, :] = ys[4 * d : 4 * d + 4]
        zown[k] = zf[0]
        zs[:, k] = zf[...].astype(BF16)
        for start, n in Z_GROUPS:

            @pl.when(k == start + n - 1)
            def _():
                for d in range(1, NZ):
                    cp_3(d, start, n).start()

    def step(i, carry):
        for lead, stage in ((LAG_D, stage_d), (LAG_C, stage_c), (LAG_B, stage_b), (0, stage_a)):
            k = i - lead

            @pl.when(jnp.logical_and(k >= 0, k < NK))
            def _():
                stage(k)

        return carry

    lax.fori_loop(0, NK + LAG_D, step, 0)

    rc(zs.at[pl.ds(1, NZ - 1)], zr.at[pl.ds(1, NZ - 1)], s_3, r_3, yp).wait_recv()

    def finish(k, carry):
        total = zown[k]
        for d in range(1, NZ):
            total = total + zr[d, k].astype(F32)
        for a in range(3):
            t = 9 * a + k
            out[t] = 0.9 * mom[t] - RATE * total[4 * a : 4 * a + 4] + 0.3 * noise[t]
        return carry

    lax.fori_loop(0, NK, finish, 0)

    def sent(ref, sem):
        rc(ref, ref, sem, sem, yp).wait_send()

    sent(W.at[pl.ds(0, 6), c, y, first], s_z.at[0])
    sent(part(4, y, first_a), s_z.at[1])
    sent(part(4, y, first_b), s_z.at[2])
    sent(W.at[:, c, y, first], s_yp)
    sent(W.at[:, c, y, first], s_ym)
    sent(W.at[:, c, y, first_a], s_hp)
    sent(W.at[:, c, y, first_b], s_hm)
    sent(W.at[0, c, pl.ds(0, 3), last], s_by)
    sent(W.at[pl.ds(0, 6), c, every, last], s_bp)
    sent(part(4, every, last), s_bm)
    sent(W.at[:, c], s_sib)

    @pl.when(seg > 0)
    def _():
        sent(upsend, s_x)

    sent(sb1, s_1)
    sent(sa, s_a)
    sent(sb, s_b)
    sent(zs.at[pl.ds(1, NZ - 1)], s_3)


def momentum_step(wt, mom, noise, act, pre, og):
    vmem = pltpu.VMEM
    dma = pltpu.SemaphoreType.DMA
    scratch = [
        vmem((27, ROWS, C), F32),
        vmem((27, ROWS, C), F32),
        vmem((MICRO * 128, C), BF16),
        vmem((MICRO * 128, C), BF16),
        vmem((MICRO * 128, C), BF16),
        dma((5,)),
        vmem((MSG, C), F32),
        vmem((NZ, 2, NY, MSG, C), BF16),
        vmem((28, C, C), BF16),
        vmem((MICRO * 128, C), F32),
        vmem((9, MICRO, 6, 32, C), BF16),
        vmem((C, MICRO * 128), BF16),
        vmem((NG, RG, C), BF16),
        vmem((NG, RG, C), BF16),
        vmem((NK, 3, 128, C), F32),
        vmem((NK, 3, 128, C), BF16),
        vmem((NK, 3, 128, C), BF16),
    ]
    scratch += [vmem((NK, 2, 3, 32, 128), BF16)] * 2
    scratch += [vmem((NK, 2, 3, 32, C), BF16)] * 2
    scratch += [
        vmem((NZ, 16, C), F32),
        vmem((NK, 16, C), F32),
        vmem((NZ, NK, 16, C), BF16),
        vmem((NZ, NK, 16, C), BF16),
    ]
    scratch += [dma((3,))] + [dma] * 14
    scratch += [dma((NZ,))] * 4 + [dma((NY,))] + [dma((NZ,))] * 2 + [dma((NG,))] + [dma((NK,))] * 3
    return pl.pallas_call(
        body,
        out_shape=jax.ShapeDtypeStruct((27, ROWS, C), F32),
        in_specs=[pl.BlockSpec(memory_space=pltpu.VMEM)] + [pl.BlockSpec(memory_space=pl.ANY)] * 5,
        out_specs=pl.BlockSpec(memory_space=pltpu.VMEM),
        scratch_shapes=scratch,
        compiler_params=pltpu.CompilerParams(
            collective_id=0, has_side_effects=True, vmem_limit_bytes=56 << 20
        ),
    )(wt, mom, noise, act, pre, og)


def shards(activations, preacts, out_grad, weights, momentum, noise):
    cells = MICRO * 128
    updated = momentum_step(
        weights[0].transpose(1, 0, 2),
        momentum[0].transpose(1, 0, 2),
        noise[0].transpose(1, 0, 2),
        activations.reshape(cells, C),
        preacts.reshape(cells, C),
        out_grad.reshape(cells, C),
    )
    return updated.transpose(1, 0, 2)[None]


def solution(mesh):
    placed = (
        P("segment", "dp", None, None, None, None),
        P("segment", "dp", None, None, None, None),
        P("dp", None, None, None, None),
        P("segment", "dp", None, None),
        P("segment", "dp", None, None),
        P("segment", "dp", None, None),
    )
    return jax.shard_map(
        shards,
        mesh=mesh,
        in_specs=placed,
        out_specs=P("segment", "dp", None, None),
        check_vma=False,
    )
```

```python
import functools
import math

import jax
import jax.numpy as jnp
from jax import lax
from jax.experimental import pallas as pl
from jax.experimental.pallas import tpu as pltpu
from jax.sharding import PartitionSpec as P

MESH = pl.DeviceIdType.MESH
F32 = jnp.float32
BF16 = jnp.bfloat16

NSEG = 4
NY = 4
NZ = 8
C = 256
ROWS = 4
MICRO = 8
G = 1
NG = MICRO // G
RATE = 1.0 / math.sqrt(NY * NZ * 2 * MICRO * 128)
RG = G * 128
MSG = 112
Z_HOPS = {
    1: (0, 1, 0, 0), 7: (0, 7, 0, 0), 2: (0, 2, 0, 0), 6: (0, 6, 0, 0), 3: (1, 2, 0, 0), 5: (7, 6, 0, 0),
    4: (2, 2, 1, 1), 12: (6, 6, 2, 2),
}
BLAG = 3
SPLIT = 96
LAG_B, LAG_C, LAG_D = 4, 8, 12

Z_GROUPS = ((0, 2), (2, 2), (4, 2), (6, 1), (7, 1), (8, 1))
NK = 9
Z_ORDER = (0, 1, 7, 2, 6, 3, 5, 4)


def iota(axis, shape=(256, 256)):
    return lax.broadcasted_iota(jnp.int32, shape, axis)


def dot(a, b, ca, cb):
    return lax.dot_general(a, b, (((ca,), (cb,)), ((), ())), preferred_element_type=F32)


def body(
    wt, mom_in, noise_in, act_in, pre_in, og_in, out,
    mom, noise, act, pre, og, s_in,
    wtmp, W, K, D, Q, XT, up, upsend,
    own1, sb1, rb1, sa, ra, sb, rb, zf, zown, zs, zr,
    s_z, s_yp, s_ym, s_hp, s_hm, s_by, s_bp, s_bm, s_sib, s_x, s_1, s_a, s_b, s_3, r_3,
    r_z, r_yp, r_ym, r_h, r_by, r_bz, r_sib, r_x, r_1, r_a, r_b,
):
    seg = lax.axis_index("segment")
    dp = lax.axis_index("dp")
    y = dp // 16
    z = (dp // 2) % 8
    c = dp % 2

    def at(yy, zz, cc):
        return (seg, yy * 16 + zz * 2 + cc)

    yp = at((y + 1) % NY, z, c)
    ym = at((y + 3) % NY, z, c)
    sib = at(y, z, 1 - c)

    def zpeer(d):
        return at(y, (z + d) % NZ, c)

    def rc(src, dst, ss, rs, dev):
        return pltpu.make_async_remote_copy(
            src_ref=src, dst_ref=dst, send_sem=ss, recv_sem=rs, device_id=dev, device_id_type=MESH
        )

    fetches = [
        pltpu.make_async_copy(src, dst, s_in.at[n])
        for n, (src, dst) in enumerate(
            ((pre_in, pre), (act_in, act), (og_in, og), (mom_in, mom), (noise_in, noise))
        )
    ]
    for fetch in fetches:
        fetch.start()

    barrier = pltpu.get_barrier_semaphore()
    peers = [yp, ym, at((y + 2) % NY, z, c), sib] + [zpeer(d) for d in (1, 7, 2, 6)]
    peers += [((seg + 1) % NSEG, dp), ((seg + NSEG - 1) % NSEG, dp)]
    for dev in peers:
        pl.semaphore_signal(barrier, inc=1, device_id=dev, device_id_type=MESH)

    wtmp[104:112, :] = jnp.zeros((8, C), F32)
    for t in range(27):
        wtmp[4 * t : 4 * t + 4, :] = wt[t]
    W[z, c, y] = wtmp[...].astype(BF16)

    for fetch in fetches:
        fetch.wait()

    Q[:, :, 0] = jnp.zeros((9, MICRO, 32, C), BF16)
    Q[:, :, 5] = jnp.zeros((9, MICRO, 32, C), BF16)

    def derivative(i, carry):
        rows = pl.ds(pl.multiple_of(i * 128, 128), 128)
        p = pre[rows, :].astype(F32)
        sig = jax.nn.sigmoid(p)
        D[rows, :] = sig * (1.0 + p * (1.0 - sig))
        return carry

    row = iota(0)
    ch = (
        ((y + ((row >> 5) & 3)) & 3) * 64
        + ((z + ((row >> 2) & 7)) & 7) * 8
        + ((c + (row >> 7)) & 1) * 4
        + (row & 3)
    )
    pick = jnp.where(iota(1) == ch, 1.0, 0.0).astype(BF16)
    XT[...] = dot(pick, act[...], 1, 1).astype(BF16)
    lax.fori_loop(0, MICRO, derivative, 0)

    pl.semaphore_wait(barrier, len(peers))

    def part(d, yy, rows):
        return W.at[(z + 8 - d) % NZ, c, yy, rows]

    first = pl.ds(0, SPLIT)
    first_a = pl.ds(0, SPLIT // 2)
    first_b = pl.ds(SPLIT // 2, SPLIT // 2)
    last = pl.ds(SPLIT, MSG - SPLIT)
    every = pl.ds(0, NY)

    def cp_z(d):
        src, by, rows, sem = Z_HOPS[d]
        piece = part(src, y, (first, first_a, first_b)[rows])
        return rc(piece, piece, s_z.at[sem], r_z.at[d % NZ], zpeer(by))

    def in_z(d):
        piece = part(d, y, first)
        return rc(piece, piece, s_z.at[0], r_z.at[d], zpeer(1))

    def cp_yp(d, src=None):
        piece = part(d, y if src is None else src, first)
        return rc(piece, piece, s_yp, r_yp.at[d], yp)

    def cp_ym(d, src=None):
        piece = part(d, y if src is None else src, first)
        return rc(piece, piece, s_ym, r_ym.at[d], ym)

    def cp_hp(d, src):
        piece = part(d, src, first_a)
        return rc(piece, piece, s_hp, r_h.at[d], yp)

    def cp_hm(d, src):
        piece = part(d, src, first_b)
        return rc(piece, piece, s_hm, r_h.at[d], ym)

    def in_h(d):
        piece = part(d, (y + 2) % NY, first)
        return rc(piece, piece, s_hp, r_h.at[d], yp)

    def cp_by(e):
        piece = part(0, y, last)
        return rc(piece, piece, s_by, r_by.at[e], at((y + e) % NY, z, c))

    def in_by(e):
        piece = part(0, (y + NY - e) % NY, last)
        return rc(piece, piece, s_by, r_by.at[e], yp)

    def cp_bz(d):
        src, by, rows, sem = Z_HOPS[d]
        piece = part(src, (every, pl.ds(0, 2), pl.ds(2, 2))[rows], last)
        return rc(piece, piece, s_bm if sem else s_bp, r_bz.at[d % 12], zpeer(by))

    def in_bz(d):
        if d == 4:
            piece = part(4, pl.ds(0, 2), last)
        elif d == 0:
            piece = part(4, pl.ds(2, 2), last)
        else:
            piece = part(d, every, last)
        return rc(piece, piece, s_bp, r_bz.at[d], zpeer(1))

    def cp_sib(d, cc):
        piece = W.at[(z + 8 - d) % NZ, cc]
        return rc(piece, piece, s_sib, r_sib.at[d], sib)

    up_of = (y + 1) % NY
    down_of = (y + 3) % NY
    for d in (1, 7, 2, 6):
        cp_z(d).start()
    cp_yp(0).start()
    cp_ym(0).start()
    for e in (1, 3, 2):
        cp_by(e).start()

    lag = len(Z_ORDER)
    for j in range(lag + 4):
        if 0 < j < lag:
            d = Z_ORDER[j]
            in_z(d).wait_recv()
            for nxt in {1: (3,), 7: (5,), 2: (4,), 6: (12,)}.get(d, ()):
                cp_z(nxt).start()
            cp_yp(d).start()
            cp_ym(d).start()
        if 0 <= j - BLAG < lag:
            d = Z_ORDER[j - BLAG]
            if d == 0:
                for e in (1, 3, 2):
                    in_by(e).wait_recv()
                for nxt in (1, 7, 2, 6):
                    cp_bz(nxt).start()
            elif d == 4:
                in_bz(4).wait_recv()
                in_bz(0).wait_recv()
            else:
                in_bz(d).wait_recv()
                for nxt in {1: (3,), 7: (5,), 2: (4,), 6: (12,)}.get(d, ()):
                    cp_bz(nxt).start()
        if 0 <= j - 2 < lag:
            d = Z_ORDER[j - 2]
            cp_yp(d, down_of).wait_recv()
            cp_hp(d, down_of).start()
            cp_ym(d, up_of).wait_recv()
            cp_hm(d, up_of).start()
        if 0 <= j - 4 < lag:
            d = Z_ORDER[j - 4]
            in_h(d).wait_recv()
            cp_sib(d, c).start()

    r = iota(0)
    src = ((r >> 3) & 1) * 128 + ((r >> 2) & 1) * 64 + ((r >> 4) & 3) * 16 + (r >> 6) * 4 + (r & 3)
    order = jnp.where(iota(1) == src, 1.0, 0.0).astype(BF16)

    def assemble(zp):
        for q in range(7):
            b = W[pl.ds(2 * zp, 2), :, :, 16 * q : 16 * q + 16, :].reshape(256, C)
            m = dot(order, b, 1, 0).astype(BF16)
            for tap in range(4):
                for yy in range(NY):
                    K[4 * q + tap, pl.ds(pl.multiple_of(64 * yy + 16 * zp, 16), 16), :] = m[
                        64 * tap + 16 * yy : 64 * tap + 16 * yy + 16
                    ]

    half_z = z // 2
    for needed, pair in (((0, 1, 7), 0), ((2, 3), 3), ((6, 5), 1), ((4,), 2)):
        for d in needed:
            cp_sib(d, 1 - c).wait_recv()

        @pl.when(seg > 0)
        def _():
            assemble((half_z + pair) % 4)

    @pl.when(jnp.logical_and(seg > 0, seg < NSEG - 1))
    def _():
        same = jnp.where(iota(0) == iota(1), 1.0, 0.0).astype(BF16)

        def turn(t, carry):
            K[t] = dot(same, K[t], 1, 1).astype(BF16)
            return carry

        lax.fori_loop(0, 27, turn, 0)

    def hop(g):
        return rc(upsend.at[g], up.at[g], s_x, r_x.at[g], (jnp.maximum(seg - 1, 0), dp))

    def pipe(g, carry):
        rows = pl.ds(pl.multiple_of(g * RG, RG), RG)

        @pl.when(seg == NSEG - 1)
        def _():
            up[g] = og[rows, :]

        @pl.when(seg < NSEG - 1)
        def _():
            hop(g).wait_recv()

        u = up[g].astype(F32)
        gp = (u * D[rows, :]).astype(BF16).astype(F32)
        cell_y = iota(0, (RG, C)) & 7
        zero = jnp.zeros((4 * G, 8, C), F32)
        for oy in (-1, 0, 1):
            if oy == 1:
                s = jnp.where(cell_y == 0, 0.0, pltpu.roll(gp, 1, 0))
            elif oy == -1:
                s = jnp.where(cell_y == 7, 0.0, pltpu.roll(gp, RG - 1, 0))
            else:
                s = gp
            s = s.reshape(4 * G, 32, C)
            for ox in (-1, 0, 1):
                if ox == 1:
                    v = jnp.concatenate([zero, s[:, :24]], axis=1)
                elif ox == -1:
                    v = jnp.concatenate([s[:, 8:], zero], axis=1)
                else:
                    v = s
                Q[3 * (ox + 1) + oy + 1, pl.ds(G * g, G), 1:5] = v.reshape(G, 4, 32, C).astype(BF16)

        def back(side):
            total = u
            for k in range(NK):
                for a in range(3):
                    q = Q[k, pl.ds(G * g, G), 2 - a : 6 - a].reshape(RG, C)
                    total = total + dot(q, K[9 * a + k], 1, side)
            upsend[g] = total.astype(BF16)
            hop(g).start()

        @pl.when(seg == NSEG - 1)
        def _():
            back(1)

        @pl.when(jnp.logical_and(seg > 0, seg < NSEG - 1))
        def _():
            back(0)

        return carry

    lax.fori_loop(0, NG, pipe, 0)

    def cp_1(k):
        return rc(sb1.at[k], rb1.at[k], s_1, r_1.at[k], sib)

    def cp_a(k, way):
        return rc(sa.at[k, way], ra.at[k, way], s_a, r_a.at[k], (yp, ym)[way])

    def in_a(k):
        return rc(sa.at[k], ra.at[k], s_a, r_a.at[k], yp)

    def cp_b(k, way):
        return rc(sb.at[k, way], rb.at[k, way], s_b, r_b.at[k], (yp, ym)[way])

    def in_b(k):
        return rc(sb.at[k], rb.at[k], s_b, r_b.at[k], yp)

    def cp_3(d, k, n):
        return rc(zs.at[d, pl.ds(k, n)], zr.at[d, pl.ds(k, n)], s_3, r_3, zpeer(d))

    for d in range(NZ):
        zf[d, 8:16, :] = jnp.zeros((8, C), F32)

    def stage_a(k):
        for a in range(3):
            g = dot(XT[...], Q[k, :, 2 - a : 6 - a].reshape(1024, C), 1, 0)
            own1[k, a] = g[:128]
            sb1[k, a] = g[128:].astype(BF16)
        cp_1(k).start()

    def stage_b(k):
        cp_1(k).wait_recv()
        total = own1[k] + rb1[k].astype(F32)
        own1[k] = total
        sa[k, 0] = total[:, 64:96, :128].astype(BF16)
        sa[k, 1] = total[:, 64:96, 128:].astype(BF16)
        cp_a(k, 0).start()
        cp_a(k, 1).start()

    def stage_c(k):
        in_a(k).wait_recv()
        sb[k, 0, :, :, :128] = (own1[k, :, 32:64, :128] + ra[k, 0].astype(F32)).astype(BF16)
        sb[k, 0, :, :, 128:] = own1[k, :, 32:64, 128:].astype(BF16)
        sb[k, 1, :, :, :128] = own1[k, :, 96:128, :128].astype(BF16)
        sb[k, 1, :, :, 128:] = (own1[k, :, 96:128, 128:] + ra[k, 1].astype(F32)).astype(BF16)
        cp_b(k, 0).start()
        cp_b(k, 1).start()

    def stage_d(k):
        in_b(k).wait_recv()
        for a in range(3):
            ys = own1[k, a, 0:32] + rb[k, 0, a].astype(F32) + rb[k, 1, a].astype(F32)
            for d in range(NZ):
                zf[d, 4 * a : 4 * a + 4, :] = ys[4 * d : 4 * d + 4]
        zown[k] = zf[0]
        zs[:, k] = zf[...].astype(BF16)
        for start, n in Z_GROUPS:

            @pl.when(k == start + n - 1)
            def _():
                for d in range(1, NZ):
                    cp_3(d, start, n).start()

    def step(i, carry):
        for lead, stage in ((LAG_D, stage_d), (LAG_C, stage_c), (LAG_B, stage_b), (0, stage_a)):
            k = i - lead

            @pl.when(jnp.logical_and(k >= 0, k < NK))
            def _():
                stage(k)

        return carry

    lax.fori_loop(0, NK + LAG_D, step, 0)

    rc(zs.at[pl.ds(1, NZ - 1)], zr.at[pl.ds(1, NZ - 1)], s_3, r_3, yp).wait_recv()

    def finish(k, carry):
        total = zown[k]
        for d in range(1, NZ):
            total = total + zr[d, k].astype(F32)
        for a in range(3):
            t = 9 * a + k
            out[t] = 0.9 * mom[t] - RATE * total[4 * a : 4 * a + 4] + 0.3 * noise[t]
        return carry

    lax.fori_loop(0, NK, finish, 0)

    def sent(ref, sem):
        rc(ref, ref, sem, sem, yp).wait_send()

    sent(W.at[pl.ds(0, 6), c, y, first], s_z.at[0])
    sent(part(4, y, first_a), s_z.at[1])
    sent(part(4, y, first_b), s_z.at[2])
    sent(W.at[:, c, y, first], s_yp)
    sent(W.at[:, c, y, first], s_ym)
    sent(W.at[:, c, y, first_a], s_hp)
    sent(W.at[:, c, y, first_b], s_hm)
    sent(W.at[0, c, pl.ds(0, 3), last], s_by)
    sent(W.at[pl.ds(0, 6), c, every, last], s_bp)
    sent(part(4, every, last), s_bm)
    sent(W.at[:, c], s_sib)

    @pl.when(seg > 0)
    def _():
        sent(upsend, s_x)

    sent(sb1, s_1)
    sent(sa, s_a)
    sent(sb, s_b)
    sent(zs.at[pl.ds(1, NZ - 1)], s_3)


def momentum_step(wt, mom, noise, act, pre, og):
    vmem = pltpu.VMEM
    dma = pltpu.SemaphoreType.DMA
    scratch = [
        vmem((27, ROWS, C), F32),
        vmem((27, ROWS, C), F32),
        vmem((MICRO * 128, C), BF16),
        vmem((MICRO * 128, C), BF16),
        vmem((MICRO * 128, C), BF16),
        dma((5,)),
        vmem((MSG, C), F32),
        vmem((NZ, 2, NY, MSG, C), BF16),
        vmem((28, C, C), BF16),
        vmem((MICRO * 128, C), F32),
        vmem((9, MICRO, 6, 32, C), BF16),
        vmem((C, MICRO * 128), BF16),
        vmem((NG, RG, C), BF16),
        vmem((NG, RG, C), BF16),
        vmem((NK, 3, 128, C), F32),
        vmem((NK, 3, 128, C), BF16),
        vmem((NK, 3, 128, C), BF16),
    ]
    scratch += [vmem((NK, 2, 3, 32, 128), BF16)] * 2
    scratch += [vmem((NK, 2, 3, 32, C), BF16)] * 2
    scratch += [
        vmem((NZ, 16, C), F32),
        vmem((NK, 16, C), F32),
        vmem((NZ, NK, 16, C), BF16),
        vmem((NZ, NK, 16, C), BF16),
    ]
    scratch += [dma((3,))] + [dma] * 14
    scratch += [dma((NZ,))] * 4 + [dma((NY,))] + [dma((NZ,))] * 2 + [dma((NG,))] + [dma((NK,))] * 3
    return pl.pallas_call(
        body,
        out_shape=jax.ShapeDtypeStruct((27, ROWS, C), F32),
        in_specs=[pl.BlockSpec(memory_space=pltpu.VMEM)] + [pl.BlockSpec(memory_space=pl.ANY)] * 5,
        out_specs=pl.BlockSpec(memory_space=pltpu.VMEM),
        scratch_shapes=scratch,
        compiler_params=pltpu.CompilerParams(
            collective_id=0, has_side_effects=True, vmem_limit_bytes=56 << 20
        ),
    )(wt, mom, noise, act, pre, og)


def shards(activations, preacts, out_grad, weights, momentum, noise):
    cells = MICRO * 128
    updated = momentum_step(
        weights[0].transpose(1, 0, 2),
        momentum[0].transpose(1, 0, 2),
        noise[0].transpose(1, 0, 2),
        activations.reshape(cells, C),
        preacts.reshape(cells, C),
        out_grad.reshape(cells, C),
    )
    return updated.transpose(1, 0, 2)[None]


def solution(mesh):
    placed = (
        P("segment", "dp", None, None, None, None),
        P("segment", "dp", None, None, None, None),
        P("dp", None, None, None, None),
        P("segment", "dp", None, None),
        P("segment", "dp", None, None),
        P("segment", "dp", None, None),
    )
    return jax.shard_map(
        shards,
        mesh=mesh,
        in_specs=placed,
        out_specs=P("segment", "dp", None, None),
        check_vma=False,
    )
```
